32 devices in a mesh: groups: 2 (over y), seq: 16 (over z, x, core).
Axes of the slice: x: 2, y: 2, z: 4, core: 2. Of those that a mesh axis runs over, the one named last changes fastest.
Arguments:
- residual: bfloat16 [8192, 1024], P(('groups', 'seq')), parts along dimension 0, may hold values from -6 to 6
- layer_queries: bfloat16 [8192, 512], P(('groups', 'seq')), parts along dimension 0, may hold values from -200 to 200
- layer_keyvals: bfloat16 [8192, 256], P(('groups', 'seq')), parts along dimension 0, may hold values from -8 to 8
- head_window_extent: int32 [8], replicated, may hold values from 32 to 256, as said below
- block_mask: int32 [16, 4], P('seq'), may hold values 0 or 1
- first_out: bfloat16 [512, 1024], replicated, may hold values from -1 to 1
- second_query: bfloat16 [1024, 512], replicated, may hold values from -12 to 12
- second_keyval: bfloat16 [1024, 256], replicated, may hold values from -1 to 1
- second_out: bfloat16 [512, 1024], replicated, may hold values from -1 to 1
Outputs:
- layer_output: bfloat16 [8192, 1024], P(('groups', 'seq')), parts along dimension 0
The draws below stay inside these ranges and needn't reach their ends.
There are 2 independent parts, one for each index of `groups`. The reference program is written for one: setup_inputs(seed, part) draws one part's arguments, and reference() takes and returns one part's arrays. A program takes and returns all parts, laid end to end along the dimension named above; an argument that names none is the same for every part. Nothing has to cross between parts.
Inputs may be any that keep to these rules, and one draw needn't show every extreme that they name: `head_window_extent`: per head; some head has exactly 256 and some exactly 32.
All inputs are finite; a program needn't handle non-finite values. No bound on the sum of `block_mask` on one device may be relied on, other than what follows from the above.
Results may differ from the reference program's by a relative error of at most 0.0065.
Values may be sent and summed in bfloat16 or wider, within the bound.
A program may use at most 64 MiB of HBM per device.

```python
import jax
import jax.numpy as jnp
from jax import lax

MODEL_WIDTH = 1024
QUERY_HEADS = 8
KEY_VALUE_HEADS = 2
HEAD_SIZE = 64
TOK_DEV = 256
WIN = 256
LEVELS = 4
NB = 16
SEQUENCE_TOKENS = 4096


def draw_pair(key):
    key_q, random_key_keys = jax.random.split(jax.random.fold_in(key, 11), 2)
    query_matrix = jnp.clip(jax.random.normal(key_q, (SEQUENCE_TOKENS, QUERY_HEADS * HEAD_SIZE), jnp.float32), -6.0, 6.0)
    key_value_pairs = jnp.clip(jax.random.normal(random_key_keys, (SEQUENCE_TOKENS, 2 * KEY_VALUE_HEADS * HEAD_SIZE), jnp.float32), -6.0, 6.0)
    return (query_matrix, key_value_pairs)


def draw_layer_queries(key, part):
    return draw_pair(key)[0].astype(jnp.bfloat16)


def draw_layer_keyvals(key, part):
    return draw_pair(key)[1].astype(jnp.bfloat16)


def draw_head_window_extent(key, part):
    key_p, key_r = jax.random.split(jax.random.fold_in(key, 31))
    order = jax.random.permutation(key_p, QUERY_HEADS)
    window_extent = jax.random.randint(key_r, (QUERY_HEADS,), WIN // 8, WIN + 1)
    window_extent = window_extent.at[order[0]].set(WIN).at[order[1]].set(WIN // 8)
    return window_extent.astype(jnp.int32)


def draw_projections(key):
    key_q, random_key_keys = jax.random.split(jax.random.fold_in(key, 23), 2)
    w_query = jnp.clip(jax.random.normal(key_q, (MODEL_WIDTH, QUERY_HEADS * HEAD_SIZE), jnp.float32), -6.0, 6.0) * MODEL_WIDTH ** (-0.5)
    key_value_weight = jnp.clip(jax.random.normal(random_key_keys, (MODEL_WIDTH, 2 * KEY_VALUE_HEADS * HEAD_SIZE), jnp.float32), -6.0, 6.0) * MODEL_WIDTH ** (-0.5)
    return (w_query, key_value_weight)


def draw_second_query(key, part):
    return draw_projections(key)[0].astype(jnp.bfloat16)


def draw_second_keyval(key, part):
    return draw_projections(key)[1].astype(jnp.bfloat16)


def set_ends(entries, stream_key, least, largest):
    longest = entries.shape.index(max(entries.shape))
    spots = []
    for shift in (0, 1):
        where = [jax.random.randint(jax.random.fold_in(stream_key, axis), (), 0, length) for axis, length in enumerate(entries.shape)]
        where[longest] = (where[longest] + shift) % entries.shape[longest]
        spots.append(tuple(where))
    return entries.at[spots[0]].set(least).at[spots[1]].set(largest)


def level_of(rng, extent, pieces, least, largest):
    def one(axis_at, parts):
        heights = jax.random.uniform(jax.random.fold_in(jax.random.fold_in(rng, 6), axis_at), (parts,), jnp.float32, least / len(pieces), largest / len(pieces))
        return jnp.repeat(jnp.exp(heights), extent[axis_at] // parts).reshape((-1,) + (1,) * (len(extent) - axis_at - 1))

    level = one(*pieces[0])
    for cut in pieces[1:]:
        level = level * one(*cut)
    return level


def centred(rng, dims, scale, most, cuts=(), kind=jnp.bfloat16):
    entries = scale * jax.random.normal(rng, dims, jnp.float32)
    if cuts:
        entries = entries * level_of(rng, dims, cuts, -0.22, 0.18)
    return jnp.clip(entries, -most, most).astype(kind)


def setup_inputs(seed: int = 0, part: int = 0) -> dict:
    keys = jax.random.split(jax.random.key(seed), 10)
    part_splits = jax.random.split(jax.random.fold_in(keys[9], part), 10)
    residual = centred(part_splits[0], (SEQUENCE_TOKENS, MODEL_WIDTH), 1.0, 6.0, ((0, 16),))
    layer_queries = draw_layer_queries(jax.random.fold_in(jax.random.fold_in(keys[9], part), 71), part)
    layer_keyvals = draw_layer_keyvals(jax.random.fold_in(jax.random.fold_in(keys[9], part), 71), part)
    head_window_extent = draw_head_window_extent(jax.random.fold_in(keys[9], 71), part)
    block_mask = set_ends((jax.random.randint(keys[4], (NB, LEVELS), 0, 4) < 3).astype(jnp.int32), jax.random.fold_in(keys[4], 1), 0, 1)
    first_out = centred(keys[5], (QUERY_HEADS * HEAD_SIZE, MODEL_WIDTH), (QUERY_HEADS * HEAD_SIZE // 16) ** -0.5, 1.0)
    second_query = draw_second_query(jax.random.fold_in(keys[9], 71), part)
    second_keyval = draw_second_keyval(jax.random.fold_in(keys[9], 71), part)
    second_out = centred(keys[8], (QUERY_HEADS * HEAD_SIZE, MODEL_WIDTH), (QUERY_HEADS * HEAD_SIZE // 16) ** -0.5, 1.0)
    return dict(residual=residual, layer_queries=layer_queries, layer_keyvals=layer_keyvals, head_window_extent=head_window_extent, block_mask=block_mask, first_out=first_out, second_query=second_query, second_keyval=second_keyval, second_out=second_out)


def norm_rows(hidden):
    values = hidden.astype(jnp.float32)
    scale = lax.rsqrt(lax.optimization_barrier(jnp.mean(values * values, axis=-1, keepdims=True)) + 1e-05)
    return (values * scale).astype(jnp.bfloat16)

def attend_rows(query_matrix, key_row_matrix, value_row_matrix, allowed):
    count_of_rows = query_matrix.shape[0]
    count_of_keys = key_row_matrix.shape[0]
    heads_per_group = QUERY_HEADS // KEY_VALUE_HEADS
    query_head_rows = query_matrix.reshape(count_of_rows, KEY_VALUE_HEADS, heads_per_group, HEAD_SIZE).astype(jnp.float32)
    key_head_rows = key_row_matrix.reshape(count_of_keys, KEY_VALUE_HEADS, HEAD_SIZE).astype(jnp.float32)
    value_head_rows = value_row_matrix.reshape(count_of_keys, KEY_VALUE_HEADS, HEAD_SIZE).astype(jnp.float32)
    scores = jnp.einsum('rkgd,jkd->kgrj', query_head_rows, key_head_rows) * HEAD_SIZE ** (-0.5)
    scores = jnp.where(allowed, scores, -1e+30)
    row_max = lax.optimization_barrier(jnp.max(scores, axis=-1, keepdims=True))
    weights = jnp.where(allowed, jnp.exp(scores - row_max), 0.0)
    shares = (weights / lax.optimization_barrier(jnp.sum(weights, axis=-1, keepdims=True))).astype(jnp.bfloat16)
    mixture = jnp.einsum('kgrj,jkd->rkgd', shares.astype(jnp.float32), value_head_rows)
    return mixture.reshape(count_of_rows, QUERY_HEADS * HEAD_SIZE).astype(jnp.bfloat16)

def reference(residual, layer_queries, layer_keyvals, head_window_extent, block_mask, first_out, second_query, second_keyval, second_out):
    key_value_width = KEY_VALUE_HEADS * HEAD_SIZE
    heads_per_group = QUERY_HEADS // KEY_VALUE_HEADS
    padded = jnp.pad(layer_keyvals, ((WIN, WIN), (0, 0)))
    window_extent = head_window_extent.reshape(KEY_VALUE_HEADS, heads_per_group, 1, 1)

    def window_block(block):
        first_row = block * TOK_DEV
        query_part = lax.dynamic_slice_in_dim(layer_queries, first_row, TOK_DEV, 0)
        key_portion = lax.dynamic_slice_in_dim(padded, first_row, TOK_DEV + 2 * WIN, 0)
        query_pos = first_row + jnp.arange(TOK_DEV, dtype=jnp.int32)
        key_pos = first_row - WIN + jnp.arange(TOK_DEV + 2 * WIN, dtype=jnp.int32)
        inside = (key_pos >= 0) & (key_pos < SEQUENCE_TOKENS)
        distance = jnp.abs(query_pos[:, None] - key_pos[None, :])
        allowed = (distance[None, None] <= window_extent) & inside[None, None, None, :]
        return attend_rows(query_part, key_portion[:, :key_value_width], key_portion[:, key_value_width:], allowed)
    attended = lax.map(window_block, jnp.arange(NB, dtype=jnp.int32)).reshape(SEQUENCE_TOKENS, QUERY_HEADS * HEAD_SIZE)
    hidden = (jnp.dot(attended, first_out, preferred_element_type=jnp.float32) + residual.astype(jnp.float32)).astype(jnp.bfloat16)
    normed = norm_rows(hidden)
    queries_two = jnp.dot(normed, second_query, preferred_element_type=jnp.float32).astype(jnp.bfloat16)
    keyvals_two = jnp.dot(normed, second_keyval, preferred_element_type=jnp.float32).astype(jnp.bfloat16)
    kv_blocks = keyvals_two.reshape(NB, TOK_DEV, 2 * key_value_width)
    level_bits = jnp.left_shift(jnp.ones((LEVELS,), jnp.int32), jnp.arange(LEVELS, dtype=jnp.int32))

    def butterfly_block(block):
        partners = jnp.bitwise_xor(block, level_bits)
        own_rows = kv_blocks[block]
        other_rows = kv_blocks[partners].reshape(LEVELS * TOK_DEV, 2 * key_value_width)
        key_portion = jnp.concatenate([own_rows, other_rows], axis=0)
        flags = jnp.concatenate([jnp.ones((1,), jnp.bool_), block_mask[block] == 1])
        allowed = jnp.repeat(flags, TOK_DEV)[None, None, None, :]
        query_part = lax.dynamic_slice_in_dim(queries_two, block * TOK_DEV, TOK_DEV, 0)
        return attend_rows(query_part, key_portion[:, :key_value_width], key_portion[:, key_value_width:], allowed)
    second = lax.map(butterfly_block, jnp.arange(NB, dtype=jnp.int32)).reshape(SEQUENCE_TOKENS, QUERY_HEADS * HEAD_SIZE)
    output = jnp.dot(second, second_out, preferred_element_type=jnp.float32) + hidden.astype(jnp.float32)
    return output.astype(jnp.bfloat16)
```

```python
import functools

import jax
import jax.numpy as jnp
from jax import lax
from jax.experimental import pallas as pl
from jax.experimental.pallas import tpu as pltpu
from jax.sharding import PartitionSpec as P

QUERY_HEADS = 8
HEAD_SIZE = 64
MESH = pl.DeviceIdType.MESH
HIDE = -1e30
TOTALS = 16
NT = (((1,), (1,)), ((), ()))


def dot_nt(a, b):
    return lax.dot_general(a, b, NT, preferred_element_type=jnp.float32)


def dot(a, b):
    return jnp.dot(a, b, preferred_element_type=jnp.float32)


def rolled(x):
    return jnp.concatenate([x[:, HEAD_SIZE:], x[:, :HEAD_SIZE]], axis=1)


def spread(keys, values, ones, kx, vt, slot):
    low = lax.broadcasted_iota(jnp.int32, keys.shape, 1) < HEAD_SIZE
    none = jnp.zeros_like(keys)
    first, second = jnp.where(low, keys, none), jnp.where(low, none, keys)
    kx[slot, 0, 0] = first
    kx[slot, 0, 1] = rolled(first)
    kx[slot, 1, 0] = rolled(second)
    kx[slot, 1, 1] = second
    for group in range(2):
        vt[slot, group, :HEAD_SIZE] = values[group * HEAD_SIZE : (group + 1) * HEAD_SIZE]
        vt[slot, group, HEAD_SIZE:] = ones


def col_max(parts):
    top = jnp.max(parts[0], axis=0, keepdims=True)
    for part in parts[1:]:
        top = jnp.maximum(top, jnp.max(part, axis=0, keepdims=True))
    return top


def weight(scores, top):
    return jnp.exp((scores - top).astype(jnp.bfloat16))


def staggered(steps, scores, weigh, finish):
    ready, weighed = {}, {}
    count = len(steps)
    for at in range(count + 2):
        if at < count:
            ready[at] = scores(steps[at])
        if 0 <= at - 1 < count:
            weighed[at - 1] = weigh(steps[at - 1], ready.pop(at - 1))
        if 0 <= at - 2 < count:
            finish(steps[at - 2], *weighed.pop(at - 2))


def shared(acc):
    return acc[:HEAD_SIZE] * (1.0 / acc[HEAD_SIZE : HEAD_SIZE + 1])


def body(
    n, levels,
    q_hbm, kv_hbm, res_hbm, extent_hbm, mask_hbm, wo1_hbm, wq2_hbm, wkv2_hbm, wo2_hbm,
    out_ref,
    q, kv, halo, res, wo1, wq2, wkv2, wo2, kv2, kv2_in, kx, vt, tops, accs, att, hid,
    extent, mask, local_sem, send_sem, recv_sem,
):
    rows = q.shape[0]
    wide = 2 * HEAD_SIZE
    pairs = q.shape[1] // wide
    per_group = pairs // 2
    scaled = jnp.bfloat16(HEAD_SIZE ** (-0.5))
    me = lax.axis_index("seq")
    loads = [
        pltpu.make_async_copy(src, dst, local_sem.at[i])
        for i, (src, dst) in enumerate(
            (
                (kv_hbm, kv),
                (q_hbm, q),
                (wo1_hbm, wo1),
                (res_hbm, res),
                (wkv2_hbm, wkv2),
                (wq2_hbm, wq2),
                (wo2_hbm, wo2),
                (extent_hbm, extent),
                (mask_hbm, mask),
            )
        )
    ]
    barrier = pltpu.get_barrier_semaphore()
    has_left, has_right = me > 0, me < n - 1

    @pl.when(has_left)
    def _():
        pl.semaphore_signal(barrier, inc=1, device_id={"seq": me - 1}, device_id_type=MESH)

    @pl.when(has_right)
    def _():
        pl.semaphore_signal(barrier, inc=1, device_id={"seq": me + 1}, device_id_type=MESH)

    def partner(level):
        bit = lax.rem(lax.div(me, 1 << level), 2)
        return me + (1 << level) * (1 - 2 * bit)

    for level in range(levels):
        pl.semaphore_signal(barrier, inc=1, device_id={"seq": partner(level)}, device_id_type=MESH)
    for load in loads:
        load.start()
    ends = has_left.astype(jnp.int32) + has_right.astype(jnp.int32)
    pl.semaphore_wait(barrier, levels + ends)

    def to_right():
        return pltpu.make_async_remote_copy(
            kv_hbm, halo.at[0], send_sem.at[0], recv_sem.at[0],
            device_id={"seq": me + 1}, device_id_type=MESH,
        )

    def to_left():
        return pltpu.make_async_remote_copy(
            kv_hbm, halo.at[1], send_sem.at[1], recv_sem.at[1],
            device_id={"seq": me - 1}, device_id_type=MESH,
        )

    @pl.when(has_right)
    def _():
        to_right().start()

    @pl.when(has_left)
    def _():
        to_left().start()

    ones = jnp.ones((TOTALS, rows), jnp.bfloat16)

    loads[0].wait()
    spread(kv[:, :wide] * scaled, kv[:, wide:].T, ones, kx, vt, 0)
    loads[1].wait()
    loads[8].wait()
    loads[7].wait()
    key = lax.broadcasted_iota(jnp.int32, (rows, rows), 0)
    query = lax.broadcasted_iota(jnp.int32, (rows, rows), 1)
    apart = jnp.abs(key - query)
    heads = list(range(2 * pairs))

    def queries_of(h):
        pair = h // 2
        return q[:, pair * wide : (pair + 1) * wide]

    def put(h, share, halves, here):
        halves.append(share)
        if h % 2:
            both = jnp.concatenate(halves, axis=0).astype(jnp.bfloat16)
            att[here, h // 2 * wide : (h // 2 + 1) * wide] = both.T
            halves.clear()

    def own_scores(h):
        return dot_nt(kx[0, h // 2 // per_group, h % 2], queries_of(h))

    def own_weigh(h, scores):
        scores = jnp.where(apart <= extent[h], scores, HIDE)
        top = col_max([scores])
        tops[h] = jnp.broadcast_to(top, tops.shape[1:])
        return (weight(scores, top),)

    def own_finish(h, shares):
        accs[h] = dot(vt[0, h // 2 // per_group], shares)

    staggered(heads, own_scores, own_weigh, own_finish)

    @pl.when(has_left)
    def _():
        to_right().wait_recv()

    @pl.when(jnp.logical_not(has_left))
    def _():
        halo[0] = jnp.zeros(halo.shape[1:], jnp.bfloat16)

    @pl.when(has_right)
    def _():
        to_left().wait_recv()

    @pl.when(jnp.logical_not(has_right))
    def _():
        halo[1] = jnp.zeros(halo.shape[1:], jnp.bfloat16)

    for side in range(2):
        spread(halo[side, :, :wide] * scaled, halo[side, :, wide:].T, ones, kx, vt, 1 + side)
    far = 4 * n * rows
    left_off = rows + jnp.where(has_left, 0, far)
    right_off = rows + jnp.where(has_right, 0, far)
    tiles = rows // wide
    for i in (2, 3, 4):
        loads[i].wait()
    swaps = [
        [
            pltpu.make_async_remote_copy(
                kv2.at[pl.ds(tile * 2 * wide, 2 * wide)],
                kv2_in.at[level, pl.ds(tile * 2 * wide, 2 * wide)],
                send_sem.at[2 + level * tiles + tile],
                recv_sem.at[2 + level * tiles + tile],
                device_id={"seq": partner(level)}, device_id_type=MESH,
            )
            for tile in range(tiles)
        ]
        for level in range(levels)
    ]
    halves, normed, turned = [], [], []
    for tile in range(tiles):
        here = slice(tile * wide, (tile + 1) * wide)
        left = slice(tile * wide, rows)
        right = slice(0, (tile + 1) * wide)
        left_apart = (query - key)[left, here] + left_off
        right_apart = (key - query)[right, here] + right_off

        def side_scores(h):
            pair = h // 2
            queries = q[here, pair * wide : (pair + 1) * wide]
            return [
                dot_nt(kx[1, pair // per_group, h % 2, left], queries),
                dot_nt(kx[2, pair // per_group, h % 2, right], queries),
            ]

        def side_weigh(h, parts):
            a = jnp.where(left_apart <= extent[h], parts[0], HIDE)
            b = jnp.where(right_apart <= extent[h], parts[1], HIDE)
            before = tops[h, 0:1, here]
            top = jnp.maximum(before, col_max([a, b]))
            return jnp.exp(before - top), weight(a, top), weight(b, top)

        def side_finish(h, fade, a, b):
            acc = accs[h, :, here] * fade
            acc += dot(vt[1, h // 2 // per_group, :, left], a)
            acc += dot(vt[2, h // 2 // per_group, :, right], b)
            put(h, shared(acc), halves, here)

        staggered(heads, side_scores, side_weigh, side_finish)

        hidden = (dot(att[here], wo1[...]) + res[here].astype(jnp.float32)).astype(jnp.bfloat16)
        hid[here] = hidden
        values = hidden.astype(jnp.float32)
        scale = lax.rsqrt(jnp.mean(values * values, axis=-1, keepdims=True) + 1e-05)
        normed.append((values * scale).astype(jnp.bfloat16))
        keyvals = dot(normed[-1], wkv2[...]).astype(jnp.bfloat16)
        turned.append(keyvals[:, wide:].T)
        kv2[tile * 2 * wide : (tile * 2 + 1) * wide] = keyvals[:, :wide] * scaled
        kv2[(tile * 2 + 1) * wide : (tile * 2 + 2) * wide] = turned[-1]
        for swap in swaps:
            swap[tile].start()

    def keys_of(block):
        return jnp.concatenate([block[2 * t * wide : (2 * t + 1) * wide] for t in range(tiles)], axis=0)

    def values_of(block):
        return jnp.concatenate(
            [block[(2 * t + 1) * wide : (2 * t + 2) * wide] for t in range(tiles)], axis=1
        )

    loads[5].wait()
    q[...] = dot(jnp.concatenate(normed, axis=0), wq2[...]).astype(jnp.bfloat16)
    spread(keys_of(kv2), values_of(kv2), ones, kx, vt, 0)

    chunks, first = [], 0
    while first <= levels:
        size = 2 if first + 1 < levels else 1
        chunks.append(list(range(first, first + size)))
        first += size
    for chunk in chunks:
        for slot in chunk:
            if slot > 0:
                for swap in swaps[slot - 1]:
                    swap.wait_recv()
                seen = mask[0, slot - 1] == 1
                came = values_of(kv2_in[slot - 1])
                spread(
                    jnp.where(seen, keys_of(kv2_in[slot - 1]), keys_of(kv2)),
                    jnp.where(seen, came, jnp.zeros_like(came)),
                    jnp.where(seen, ones, jnp.zeros_like(ones)),
                    kx, vt, slot,
                )

        def far_scores(h):
            return [dot_nt(kx[slot, h // 2 // per_group, h % 2], queries_of(h)) for slot in chunk]

        def far_weigh(h, parts):
            top = col_max(parts)
            fade = None
            if chunk[0] > 0:
                before = tops[h, 0:1]
                top = jnp.maximum(before, top)
                fade = jnp.exp(before - top)
            if chunk[-1] < levels:
                tops[h] = jnp.broadcast_to(top, tops.shape[1:])
            return fade, [weight(part, top) for part in parts]

        def far_finish(h, fade, parts):
            acc = None if fade is None else accs[h] * fade
            for slot, part in zip(chunk, parts):
                term = dot(vt[slot, h // 2 // per_group], part)
                acc = term if acc is None else acc + term
            if chunk[-1] < levels:
                accs[h] = acc
            else:
                put(h, shared(acc), halves, slice(0, rows))

        staggered(heads, far_scores, far_weigh, far_finish)

    loads[6].wait()
    final = (dot(att[...], wo2[...]) + hid[...].astype(jnp.float32)).astype(jnp.bfloat16)
    out_ref[...] = final
    for level in swaps:
        for swap in level:
            swap.wait_send()

    @pl.when(has_right)
    def _():
        to_right().wait_send()

    @pl.when(has_left)
    def _():
        to_left().wait_send()


def shards(
    n, residual, layer_queries, layer_keyvals, head_window_extent, block_mask,
    first_out, second_query, second_keyval, second_out,
):
    levels = n.bit_length() - 1
    rows, width = residual.shape
    query_width = layer_queries.shape[1]
    kv_width = layer_keyvals.shape[1]
    wide = 2 * HEAD_SIZE
    blocks = max(3, levels + 1)
    bf16, f32 = jnp.bfloat16, jnp.float32
    anywhere = pl.BlockSpec(memory_space=pl.ANY)
    stays = pl.BlockSpec(memory_space=pltpu.HBM)
    scalars = pl.BlockSpec(memory_space=pltpu.SMEM)
    return pl.pallas_call(
        functools.partial(body, n, levels),
        name="two_layers",
        out_shape=pltpu.VMEM((rows, width), bf16),
        in_specs=[stays] * 9,
        out_specs=pl.BlockSpec(memory_space=pltpu.VMEM),
        scratch_shapes=[
            pltpu.VMEM((rows, query_width), bf16),
            pltpu.VMEM((rows, kv_width), bf16),
            pltpu.VMEM((2, rows, kv_width), bf16),
            pltpu.VMEM((rows, width), bf16),
            pltpu.VMEM(first_out.shape, bf16),
            pltpu.VMEM(second_query.shape, bf16),
            pltpu.VMEM(second_keyval.shape, bf16),
            pltpu.VMEM(second_out.shape, bf16),
            pltpu.VMEM((2 * rows, wide), bf16),
            pltpu.VMEM((levels, 2 * rows, wide), bf16),
            pltpu.VMEM((blocks, 2, 2, rows, wide), bf16),
            pltpu.VMEM((blocks, 2, HEAD_SIZE + TOTALS, rows), bf16),
            pltpu.VMEM((QUERY_HEADS, 8, rows), f32),
            pltpu.VMEM((QUERY_HEADS, HEAD_SIZE + TOTALS, rows), f32),
            pltpu.VMEM((rows, query_width), bf16),
            pltpu.VMEM((rows, width), bf16),
            pltpu.SMEM(head_window_extent.shape, jnp.int32),
            pltpu.SMEM(block_mask.shape, jnp.int32),
            pltpu.SemaphoreType.DMA((10,)),
            pltpu.SemaphoreType.DMA((2 + levels * (rows // wide),)),
            pltpu.SemaphoreType.DMA((2 + levels * (rows // wide),)),
        ],
        compiler_params=pltpu.CompilerParams(
            collective_id=0, has_side_effects=True
        ),
    )(
        layer_queries, layer_keyvals, residual, head_window_extent, block_mask,
        first_out, second_query, second_keyval, second_out,
    )


def solution(mesh):
    placed = (
        P(("groups", "seq"), None),
        P(("groups", "seq"), None),
        P(("groups", "seq"), None),
        P(),
        P("seq", None),
        P(),
        P(),
        P(),
        P(),
    )
    return jax.shard_map(
        functools.partial(shards, mesh.shape["seq"]),
        mesh=mesh, in_specs=placed, out_specs=P(("groups", "seq"), None), check_vma=False,
    )
```

```python
import functools

import jax
import jax.numpy as jnp
from jax import lax
from jax.experimental import pallas as pl
from jax.experimental.pallas import tpu as pltpu
from jax.sharding import PartitionSpec as P

QUERY_HEADS = 8
HEAD_SIZE = 64
WIDE = 2 * HEAD_SIZE
MESH = pl.DeviceIdType.MESH
HIDE = -1e30
TOTALS = 16
NT = (((1,), (1,)), ((), ()))


def dot_nt(a, b):
    return lax.dot_general(a, b, NT, preferred_element_type=jnp.float32)


def dot(a, b):
    return jnp.dot(a, b, preferred_element_type=jnp.float32)


def col_max(parts):
    top = jnp.max(parts[0], axis=0, keepdims=True)
    for part in parts[1:]:
        top = jnp.maximum(top, jnp.max(part, axis=0, keepdims=True))
    return top


def weight(scores, top):
    return jnp.exp((scores - top).astype(jnp.bfloat16))


def staggered(steps, scores, weigh, finish):
    ready, weighed = {}, {}
    count = len(steps)
    for at in range(count + 2):
        if at < count:
            ready[at] = scores(steps[at])
        if 0 <= at - 1 < count:
            weighed[at - 1] = weigh(steps[at - 1], ready.pop(at - 1))
        if 0 <= at - 2 < count:
            finish(steps[at - 2], *weighed.pop(at - 2))


def shared(acc):
    return acc[:HEAD_SIZE] * (1.0 / acc[HEAD_SIZE : HEAD_SIZE + 1])


def body(
    n, levels,
    q_hbm, kv_hbm, res_hbm, extent_hbm, mask_hbm, wo1_hbm, wq2_hbm, wkv2_hbm, wo2_hbm,
    out_ref,
    q, kv, res, wo1, wq2, wkv2, wo2, qx, halo, own2, came, kb, vt, tops, accs, att, hid, norm,
    extent, mask, local_sem, send_sem, recv_sem, enter_sem,
):
    rows = q.shape[0]
    tiles = rows // WIDE
    pairs = q.shape[1] // WIDE
    group_heads = pairs
    heads = list(range(2 * pairs))
    bf16, f32 = jnp.bfloat16, jnp.float32
    scaled = bf16(HEAD_SIZE ** (-0.5))
    me = lax.axis_index("seq")
    loads = {
        name: pltpu.make_async_copy(src, dst, local_sem.at[i])
        for i, (name, src, dst) in enumerate(
            (
                ("kv", kv_hbm, kv),
                ("q", q_hbm, q),
                ("extent", extent_hbm, extent),
                ("mask", mask_hbm, mask),
                ("wo1", wo1_hbm, wo1),
                ("res", res_hbm, res),
                ("wkv2", wkv2_hbm, wkv2),
                ("wq2", wq2_hbm, wq2),
                ("wo2", wo2_hbm, wo2),
            )
        )
    }
    barrier = pltpu.get_barrier_semaphore()
    has_left, has_right = me > 0, me < n - 1

    def partner(level):
        bit = lax.rem(lax.div(me, 1 << level), 2)
        return me + (1 << level) * (1 - 2 * bit)

    def tell(sem, reach):
        @pl.when(me >= reach)
        def _():
            pl.semaphore_signal(sem, inc=1, device_id={"seq": me - reach}, device_id_type=MESH)

        @pl.when(me < n - reach)
        def _():
            pl.semaphore_signal(sem, inc=1, device_id={"seq": me + reach}, device_id_type=MESH)

    def told(sem, reach):
        pl.semaphore_wait(sem, (me >= reach).astype(jnp.int32) + (me < n - reach).astype(jnp.int32))

    tell(barrier, 1)
    for load in loads.values():
        load.start()

    def to_right(near):
        slot = 1 if near else 0
        return pltpu.make_async_remote_copy(
            kv_hbm.at[pl.ds(slot * WIDE, WIDE)], halo.at[slot], send_sem.at[slot], recv_sem.at[slot],
            device_id={"seq": me + 1}, device_id_type=MESH,
        )

    def to_left(near):
        slot = 2 if near else 3
        return pltpu.make_async_remote_copy(
            kv_hbm.at[pl.ds((slot - 2) * WIDE, WIDE)], halo.at[slot], send_sem.at[slot], recv_sem.at[slot],
            device_id={"seq": me - 1}, device_id_type=MESH,
        )

    told(barrier, 1)
    for near in (True, False):

        @pl.when(has_right)
        def _():
            to_right(near).start()

        @pl.when(has_left)
        def _():
            to_left(near).start()

    stages = max(levels - 1, 0)

    def go_on(stage):
        if stage < stages:
            told(enter_sem.at[stage], 1 << stage)
            if stage + 1 < stages:
                tell(enter_sem.at[stage + 1], 1 << (stage + 1))

    if stages:
        tell(enter_sem.at[0], 1)

    for piece in range(vt.shape[0]):
        for group in range(2):
            vt[piece, group, HEAD_SIZE:] = jnp.ones((TOTALS, WIDE), bf16)

    @pl.when(jnp.logical_not(has_left))
    def _():
        halo[0:2] = jnp.zeros((2, *halo.shape[1:]), bf16)

    @pl.when(jnp.logical_not(has_right))
    def _():
        halo[2:4] = jnp.zeros((2, *halo.shape[1:]), bf16)

    def values_in(piece, turned):
        for group in range(2):
            vt[piece, group, :HEAD_SIZE] = turned[group * HEAD_SIZE : (group + 1) * HEAD_SIZE]

    def spread_queries(block):
        low = lax.broadcasted_iota(jnp.int32, (rows, WIDE), 1) < HEAD_SIZE
        none = jnp.zeros((rows, WIDE), bf16)
        for h in heads:
            pair = block[:, h // 2 * WIDE : (h // 2 + 1) * WIDE]
            group = h // group_heads
            if h % 2 != group:
                pair = jnp.concatenate([pair[:, HEAD_SIZE:], pair[:, :HEAD_SIZE]], axis=1)
            qx[h] = jnp.where(low, pair, none) if group == 0 else jnp.where(low, none, pair)

    loads["kv"].wait()
    for t in range(tiles):
        values_in(t, kv[t * WIDE : (t + 1) * WIDE, WIDE:].T)
    loads["q"].wait()
    loads["extent"].wait()
    loads["mask"].wait()
    spread_queries(q[...] * scaled)

    def both(pieces, ref, group):
        return jnp.concatenate([ref[p, group] for p in pieces], axis=1)

    key = lax.broadcasted_iota(jnp.int32, (rows, rows), 0)
    query = lax.broadcasted_iota(jnp.int32, (rows, rows), 1)
    apart = jnp.abs(key - query)

    def own_scores(h):
        return [dot_nt(kv[t * WIDE : (t + 1) * WIDE, :WIDE], qx[h]) for t in range(tiles)]

    def own_weigh(h, parts):
        parts = [
            jnp.where(apart[t * WIDE : (t + 1) * WIDE] <= extent[h], part, HIDE)
            for t, part in enumerate(parts)
        ]
        top = col_max(parts)
        for t in range(tiles):
            tops[t, h] = jnp.broadcast_to(top[:, t * WIDE : (t + 1) * WIDE], tops.shape[2:])
        return (jnp.concatenate([weight(part, top) for part in parts], axis=0),)

    def own_finish(h, shares):
        acc = dot(both(range(tiles), vt, h // group_heads), shares)
        for t in range(tiles):
            accs[t, h] = acc[:, t * WIDE : (t + 1) * WIDE]

    half = len(heads) // 2
    staggered(heads[:half], own_scores, own_weigh, own_finish)
    go_on(0)
    staggered(heads[half:], own_scores, own_weigh, own_finish)
    go_on(1)

    @pl.when(has_left)
    def _():
        to_right(True).wait_recv()

    @pl.when(has_right)
    def _():
        to_left(True).wait_recv()

    for piece in (1, 2):
        values_in(tiles + piece, halo[piece, :, WIDE:].T)

    parity = lax.rem(me, 2)
    order = (1 - parity, parity)
    far = 4 * n * rows
    left_off = jnp.where(has_left, 0, far)
    right_off = jnp.where(has_right, 0, far)
    delta = (
        lax.broadcasted_iota(jnp.int32, (WIDE, WIDE), 1)
        - lax.broadcasted_iota(jnp.int32, (WIDE, WIDE), 0)
    )
    swaps = [
        [
            pltpu.make_async_remote_copy(
                own2.at[t], came.at[level, t],
                send_sem.at[4 + level * tiles + t], recv_sem.at[4 + level * tiles + t],
                device_id={"seq": partner(level)}, device_id_type=MESH,
            )
            for t in order
        ]
        for level in range(levels)
    ]
    halves = []

    def put(h, share, where_to):
        halves.append(share)
        if h % 2:
            pair = jnp.concatenate(halves, axis=0).astype(bf16)
            att[where_to, h // 2 * WIDE : (h // 2 + 1) * WIDE] = pair.T
            halves.clear()

    for name in ("wo1", "res", "wkv2"):
        loads[name].wait()
    for step, t in enumerate(order):
        here = pl.ds(pl.multiple_of(t * WIDE, WIDE), WIDE)
        at_left = t == 0

        @pl.when(jnp.logical_and(at_left, has_left))
        def _():
            to_right(False).wait_recv()

        @pl.when(jnp.logical_and(jnp.logical_not(at_left), has_right))
        def _():
            to_left(False).wait_recv()

        far_piece = 3 * t
        values_in(tiles + far_piece, halo[far_piece, :, WIDE:].T)
        sign = 1 - 2 * t
        off_mid = jnp.where(at_left, left_off, right_off)
        middle = delta * sign

        def side_scores(h):
            return [dot_nt(halo[t + i, :, :WIDE], qx[h, here]) for i in range(3)]

        def side_weigh(h, parts):
            reach = extent[h]
            a = jnp.where(delta <= reach - rows - left_off, parts[0], HIDE)
            b = jnp.where(middle <= reach - WIDE - off_mid, parts[1], HIDE)
            c = jnp.where(delta >= rows + right_off - reach, parts[2], HIDE)
            before = tops[t, h, 0:1]
            top = jnp.maximum(before, col_max([a, b, c]))
            return jnp.exp(before - top), jnp.concatenate([weight(x, top) for x in (a, b, c)], axis=0)

        def side_finish(h, fade, shares):
            lhs = both([tiles + t + i for i in range(3)], vt, h // group_heads)
            put(h, shared(accs[t, h] * fade + dot(lhs, shares)), here)

        staggered(heads, side_scores, side_weigh, side_finish)

        hidden = (dot(att[here], wo1[...]) + res[here].astype(f32)).astype(bf16)
        hid[here] = hidden
        values = hidden.astype(f32)
        scale = lax.rsqrt(jnp.mean(values * values, axis=-1, keepdims=True) + 1e-05)
        normed = (values * scale).astype(bf16)
        norm[here] = normed
        keyvals = dot(normed, wkv2[...]).astype(bf16)
        own2[t, :WIDE] = keyvals[:, :WIDE]
        own2[t, WIDE:] = keyvals[:, WIDE:].T
        if step == 0:
            for stage in range(2, stages):
                go_on(stage)
        for swap in reversed(swaps):
            swap[step].start()

    loads["wq2"].wait()
    spread_queries(dot(norm[...], wq2[...]).astype(bf16) * scaled)

    first = [(0, t) for t in range(tiles)]
    chunks = [first]
    if levels > 0:
        chunks = [first + [(1, t) for t in range(tiles)]]
    split = max(1, levels - 2)
    for level in range(1, split):
        chunks.append([(level + 1, t) for t in range(tiles)])
    if levels > split:
        for t in order:
            chunks.append([(level + 1, t) for level in reversed(range(split, levels))])
    last = len(chunks) - 1

    for number, chunk in enumerate(chunks):
        for slot, t in chunk:
            if slot == 0:
                values_in(t, own2[t, WIDE:])
                continue
            level = slot - 1
            pltpu.make_async_remote_copy(
                own2.at[t], came.at[level, t],
                send_sem.at[4 + level * tiles + t], recv_sem.at[4 + level * tiles + t],
                device_id={"seq": partner(level)}, device_id_type=MESH,
            ).wait_recv()
            seen = mask[0, level] == 1
            piece = slot * tiles + t
            kb[level * tiles + t] = jnp.where(seen, came[level, t, :WIDE], own2[t, :WIDE])
            turned = came[level, t, WIDE:]
            values_in(piece, jnp.where(seen, turned, jnp.zeros_like(turned)))
            for group in range(2):
                vt[piece, group, HEAD_SIZE:] = jnp.where(
                    seen, jnp.ones((TOTALS, WIDE), bf16), jnp.zeros((TOTALS, WIDE), bf16)
                )

        def keys_of(slot, t):
            return own2[t, :WIDE] if slot == 0 else kb[(slot - 1) * tiles + t]

        def far_scores(h):
            return [dot_nt(keys_of(slot, t), qx[h]) for slot, t in chunk]

        def far_weigh(h, parts):
            top = col_max(parts)
            fade = None
            if number > 0:
                before = jnp.concatenate([tops[t, h, 0:1] for t in range(tiles)], axis=1)
                top = jnp.maximum(before, top)
                fade = jnp.exp(before - top)
            if number < last:
                for t in range(tiles):
                    tops[t, h] = jnp.broadcast_to(top[:, t * WIDE : (t + 1) * WIDE], tops.shape[2:])
            return fade, [weight(part, top) for part in parts]

        def far_finish(h, fade, parts):
            acc = None
            if fade is not None:
                acc = jnp.concatenate([accs[t, h] for t in range(tiles)], axis=1) * fade
            for i in range(0, len(chunk), 2):
                lhs = both([slot * tiles + t for slot, t in chunk[i : i + 2]], vt, h // group_heads)
                term = dot(lhs, jnp.concatenate(parts[i : i + 2], axis=0))
                acc = term if acc is None else acc + term
            if number < last:
                for t in range(tiles):
                    accs[t, h] = acc[:, t * WIDE : (t + 1) * WIDE]
            else:
                put(h, shared(acc), slice(0, rows))

        staggered(heads, far_scores, far_weigh, far_finish)

    loads["wo2"].wait()
    out_ref[...] = (dot(att[...], wo2[...]) + hid[...].astype(f32)).astype(bf16)
    for level in swaps:
        for swap in level:
            swap.wait_send()
    for near in (True, False):

        @pl.when(has_right)
        def _():
            to_right(near).wait_send()

        @pl.when(has_left)
        def _():
            to_left(near).wait_send()


def shards(
    n, residual, layer_queries, layer_keyvals, head_window_extent, block_mask,
    first_out, second_query, second_keyval, second_out,
):
    levels = n.bit_length() - 1
    rows, width = residual.shape
    query_width = layer_queries.shape[1]
    kv_width = layer_keyvals.shape[1]
    tiles = rows // WIDE
    pieces = max(tiles + 4, (levels + 1) * tiles)
    bf16, f32 = jnp.bfloat16, jnp.float32
    stays = pl.BlockSpec(memory_space=pltpu.HBM)
    return pl.pallas_call(
        functools.partial(body, n, levels),
        name="two_layers",
        out_shape=pltpu.VMEM((rows, width), bf16),
        in_specs=[stays] * 9,
        out_specs=pl.BlockSpec(memory_space=pltpu.VMEM),
        scratch_shapes=[
            pltpu.VMEM((rows, query_width), bf16),
            pltpu.VMEM((rows, kv_width), bf16),
            pltpu.VMEM((rows, width), bf16),
            pltpu.VMEM(first_out.shape, bf16),
            pltpu.VMEM(second_query.shape, bf16),
            pltpu.VMEM(second_keyval.shape, bf16),
            pltpu.VMEM(second_out.shape, bf16),
            pltpu.VMEM((QUERY_HEADS, rows, WIDE), bf16),
            pltpu.VMEM((4, WIDE, kv_width), bf16),
            pltpu.VMEM((tiles, 2 * WIDE, WIDE), bf16),
            pltpu.VMEM((max(levels, 1), tiles, 2 * WIDE, WIDE), bf16),
            pltpu.VMEM((max(levels, 1) * tiles, WIDE, WIDE), bf16),
            pltpu.VMEM((pieces, 2, HEAD_SIZE + TOTALS, WIDE), bf16),
            pltpu.VMEM((tiles, QUERY_HEADS, 8, WIDE), f32),
            pltpu.VMEM((tiles, QUERY_HEADS, HEAD_SIZE + TOTALS, WIDE), f32),
            pltpu.VMEM((rows, query_width), bf16),
            pltpu.VMEM((rows, width), bf16),
            pltpu.VMEM((rows, width), bf16),
            pltpu.SMEM(head_window_extent.shape, jnp.int32),
            pltpu.SMEM(block_mask.shape, jnp.int32),
            pltpu.SemaphoreType.DMA((9,)),
            pltpu.SemaphoreType.DMA((4 + levels * tiles,)),
            pltpu.SemaphoreType.DMA((4 + levels * tiles,)),
            pltpu.SemaphoreType.REGULAR((max(levels - 1, 1),)),
        ],
        compiler_params=pltpu.CompilerParams(
            collective_id=0, has_side_effects=True
        ),
    )(
        layer_queries, layer_keyvals, residual, head_window_extent, block_mask,
        first_out, second_query, second_keyval, second_out,
    )


def solution(mesh):
    placed = (
        P(("groups", "seq"), None),
        P(("groups", "seq"), None),
        P(("groups", "seq"), None),
        P(),
        P("seq", None),
        P(),
        P(),
        P(),
        P(),
    )
    return jax.shard_map(
        functools.partial(shards, mesh.shape["seq"]),
        mesh=mesh, in_specs=placed, out_specs=P(("groups", "seq"), None), check_vma=False,
    )
```

```python
import functools

import jax
import jax.numpy as jnp
from jax import lax
from jax.experimental import pallas as pl
from jax.experimental.pallas import tpu as pltpu
from jax.sharding import PartitionSpec as P

QUERY_HEADS = 8
HEAD_SIZE = 64
WIDE = 2 * HEAD_SIZE
MESH = pl.DeviceIdType.MESH
HIDE = -1e30
TOTALS = 16


def dot(a, b):
    return jnp.dot(a, b, preferred_element_type=jnp.float32)


def col_max(parts):
    top = jnp.max(parts[0], axis=0, keepdims=True)
    for part in parts[1:]:
        top = jnp.maximum(top, jnp.max(part, axis=0, keepdims=True))
    return top


def weight(scores, top):
    return jnp.exp((scores - top).astype(jnp.bfloat16))


def staggered(steps, scores, weigh, finish):
    ready, weighed = {}, {}
    count = len(steps)
    for at in range(count + 2):
        if at < count:
            ready[at] = scores(steps[at])
        if 0 <= at - 1 < count:
            weighed[at - 1] = weigh(steps[at - 1], ready.pop(at - 1))
        if 0 <= at - 2 < count:
            finish(steps[at - 2], *weighed.pop(at - 2))


def shared(acc):
    return acc[:HEAD_SIZE] * (1.0 / acc[HEAD_SIZE : HEAD_SIZE + 1])


def body(
    n, levels,
    q_hbm, kv_hbm, res_hbm, extent_hbm, mask_hbm, wo1_hbm, wq2_hbm, wkv2_hbm, wo2_hbm,
    out_ref,
    q, kv, res, wo1, wq2, wkv2, wo2, qx, halo, own2, came, kb, vt, tops, accs, att, hid, norm,
    extent, mask, local_sem, send_sem, recv_sem, enter_sem,
):
    rows = q.shape[0]
    tiles = rows // WIDE
    pairs = q.shape[1] // WIDE
    group_heads = pairs
    heads = list(range(2 * pairs))
    bf16, f32 = jnp.bfloat16, jnp.float32
    scaled = bf16(HEAD_SIZE ** (-0.5))
    me = lax.axis_index("seq")
    loads = {
        name: pltpu.make_async_copy(src, dst, local_sem.at[i])
        for i, (name, src, dst) in enumerate(
            (
                ("kv", kv_hbm, kv),
                ("q", q_hbm, q),
                ("extent", extent_hbm, extent),
                ("mask", mask_hbm, mask),
                ("wo1", wo1_hbm, wo1),
                ("res", res_hbm, res),
                ("wkv2", wkv2_hbm, wkv2),
                ("wq2", wq2_hbm, wq2),
                ("wo2", wo2_hbm, wo2),
            )
        )
    }
    barrier = pltpu.get_barrier_semaphore()
    has_left, has_right = me > 0, me < n - 1

    def partner(level):
        bit = lax.rem(lax.div(me, 1 << level), 2)
        return me + (1 << level) * (1 - 2 * bit)

    def tell(sem, reach):
        @pl.when(me >= reach)
        def _():
            pl.semaphore_signal(sem, inc=1, device_id={"seq": me - reach}, device_id_type=MESH)

        @pl.when(me < n - reach)
        def _():
            pl.semaphore_signal(sem, inc=1, device_id={"seq": me + reach}, device_id_type=MESH)

    def told(sem, reach):
        pl.semaphore_wait(sem, (me >= reach).astype(jnp.int32) + (me < n - reach).astype(jnp.int32))

    tell(barrier, 1)
    for load in loads.values():
        load.start()

    def to_right(near):
        slot = 1 if near else 0
        return pltpu.make_async_remote_copy(
            kv_hbm.at[pl.ds(slot * WIDE, WIDE)], halo.at[slot], send_sem.at[slot], recv_sem.at[slot],
            device_id={"seq": me + 1}, device_id_type=MESH,
        )

    def to_left(near):
        slot = 2 if near else 3
        return pltpu.make_async_remote_copy(
            kv_hbm.at[pl.ds((slot - 2) * WIDE, WIDE)], halo.at[slot], send_sem.at[slot], recv_sem.at[slot],
            device_id={"seq": me - 1}, device_id_type=MESH,
        )

    told(barrier, 1)
    for near in (True, False):

        @pl.when(has_right)
        def _():
            to_right(near).start()

        @pl.when(has_left)
        def _():
            to_left(near).start()

    stages = max(levels - 1, 0)

    def go_on(stage):
        if stage < stages:
            told(enter_sem.at[stage], 1 << stage)
            if stage + 1 < stages:
                tell(enter_sem.at[stage + 1], 1 << (stage + 1))

    if stages:
        tell(enter_sem.at[0], 1)

    for piece in range(vt.shape[0]):
        for group in range(2):
            vt[piece, group, HEAD_SIZE:] = jnp.ones((TOTALS, WIDE), bf16)

    @pl.when(jnp.logical_not(has_left))
    def _():
        halo[0:2] = jnp.zeros((2, *halo.shape[1:]), bf16)

    @pl.when(jnp.logical_not(has_right))
    def _():
        halo[2:4] = jnp.zeros((2, *halo.shape[1:]), bf16)

    def values_in(piece, turned):
        for group in range(2):
            vt[piece, group, :HEAD_SIZE] = turned[group * HEAD_SIZE : (group + 1) * HEAD_SIZE]

    def spread_queries(block):
        for pair in range(pairs):
            for t in range(tiles):
                turned = block[t * WIDE : (t + 1) * WIDE, pair * WIDE : (pair + 1) * WIDE].T
                for h in (2 * pair, 2 * pair + 1):
                    group = h // group_heads
                    start = group * HEAD_SIZE
                    qx[t, h, start : start + HEAD_SIZE] = turned[h % 2 * HEAD_SIZE : (h % 2 + 1) * HEAD_SIZE]

    for h in heads:
        start = (1 - h // group_heads) * HEAD_SIZE
        qx[:, h, start : start + HEAD_SIZE] = jnp.zeros((tiles, HEAD_SIZE, WIDE), bf16)

    def queries_of(h):
        return jnp.concatenate([qx[t, h] for t in range(tiles)], axis=1)

    loads["kv"].wait()
    for t in range(tiles):
        values_in(t, kv[t * WIDE : (t + 1) * WIDE, WIDE:].T)
    loads["q"].wait()
    loads["extent"].wait()
    loads["mask"].wait()
    spread_queries(q[...] * scaled)

    def both(pieces, ref, group):
        return jnp.concatenate([ref[p, group] for p in pieces], axis=1)

    key = lax.broadcasted_iota(jnp.int32, (rows, rows), 0)
    query = lax.broadcasted_iota(jnp.int32, (rows, rows), 1)
    apart = jnp.abs(key - query)

    def own_scores(h):
        return (dot(kv[:, :WIDE], queries_of(h)),)

    def own_weigh(h, parts):
        scores = jnp.where(apart <= extent[h], parts[0], HIDE)
        top = col_max([scores])
        for t in range(tiles):
            tops[t, h] = jnp.broadcast_to(top[:, t * WIDE : (t + 1) * WIDE], tops.shape[2:])
        return (weight(scores, top),)

    def own_finish(h, shares):
        acc = dot(both(range(tiles), vt, h // group_heads), shares)
        for t in range(tiles):
            accs[t, h] = acc[:, t * WIDE : (t + 1) * WIDE]

    half = len(heads) // 2
    staggered(heads[:half], own_scores, own_weigh, own_finish)
    go_on(0)
    staggered(heads[half:], own_scores, own_weigh, own_finish)
    go_on(1)

    @pl.when(has_left)
    def _():
        to_right(True).wait_recv()

    @pl.when(has_right)
    def _():
        to_left(True).wait_recv()

    for piece in (1, 2):
        values_in(tiles + piece, halo[piece, :, WIDE:].T)

    parity = lax.rem(me, 2)
    order = (1 - parity, parity)
    far = 4 * n * rows
    left_off = jnp.where(has_left, 0, far)
    right_off = jnp.where(has_right, 0, far)
    delta = (
        lax.broadcasted_iota(jnp.int32, (WIDE, WIDE), 1)
        - lax.broadcasted_iota(jnp.int32, (WIDE, WIDE), 0)
    )
    swaps = [
        [
            pltpu.make_async_remote_copy(
                own2.at[t], came.at[level, t],
                send_sem.at[4 + level * tiles + t], recv_sem.at[4 + level * tiles + t],
                device_id={"seq": partner(level)}, device_id_type=MESH,
            )
            for t in order
        ]
        for level in range(levels)
    ]
    halves = []

    def put(h, share, where_to):
        halves.append(share)
        if h % 2:
            pair = jnp.concatenate(halves, axis=0).astype(bf16)
            att[where_to, h // 2 * WIDE : (h // 2 + 1) * WIDE] = pair.T
            halves.clear()

    for name in ("wo1", "res", "wkv2"):
        loads[name].wait()
    for step, t in enumerate(order):
        here = pl.ds(pl.multiple_of(t * WIDE, WIDE), WIDE)
        at_left = t == 0

        @pl.when(jnp.logical_and(at_left, has_left))
        def _():
            to_right(False).wait_recv()

        @pl.when(jnp.logical_and(jnp.logical_not(at_left), has_right))
        def _():
            to_left(False).wait_recv()

        far_piece = 3 * t
        values_in(tiles + far_piece, halo[far_piece, :, WIDE:].T)
        sign = 1 - 2 * t
        off_mid = jnp.where(at_left, left_off, right_off)
        middle = delta * sign

        def twice(ref, h):
            return jnp.concatenate([ref[t, h], ref[t, h + 1]], axis=1)

        def side_scores(h):
            keys = jnp.concatenate([halo[t + i, :, :WIDE] for i in range(3)], axis=0)
            scores = dot(keys, twice(qx, h))
            return [scores[i * WIDE : (i + 1) * WIDE] for i in range(3)]

        def side_weigh(h, parts):
            kept = []
            for k in range(2):
                reach = extent[h + k]
                a, b, c = (part[:, k * WIDE : (k + 1) * WIDE] for part in parts)
                kept.append((
                    jnp.where(delta <= reach - rows - left_off, a, HIDE),
                    jnp.where(middle <= reach - WIDE - off_mid, b, HIDE),
                    jnp.where(delta >= rows + right_off - reach, c, HIDE),
                ))
            shares, fades = [], []
            for k in range(2):
                before = tops[t, h + k, 0:1]
                top = jnp.maximum(before, col_max(kept[k]))
                fades.append(jnp.exp(before - top))
                shares.append(jnp.concatenate([weight(x, top) for x in kept[k]], axis=0))
            return jnp.concatenate(fades, axis=1), jnp.concatenate(shares, axis=1)

        def side_finish(h, fade, shares):
            lhs = both([tiles + t + i for i in range(3)], vt, h // group_heads)
            acc = twice(accs, h) * fade + dot(lhs, shares)
            for k in range(2):
                put(h + k, shared(acc[:, k * WIDE : (k + 1) * WIDE]), here)

        staggered(heads[::2], side_scores, side_weigh, side_finish)

        hidden = (dot(att[here], wo1[...]) + res[here].astype(f32)).astype(bf16)
        hid[here] = hidden
        values = hidden.astype(f32)
        scale = lax.rsqrt(jnp.mean(values * values, axis=-1, keepdims=True) + 1e-05)
        normed = (values * scale).astype(bf16)
        norm[here] = normed
        keyvals = dot(normed, wkv2[...]).astype(bf16)
        own2[t, :WIDE] = keyvals[:, :WIDE]
        own2[t, WIDE:] = keyvals[:, WIDE:].T
        if step == 0:
            for stage in range(2, stages):
                go_on(stage)
        for swap in reversed(swaps):
            swap[step].start()

    loads["wq2"].wait()
    spread_queries(dot(norm[...], wq2[...]).astype(bf16) * scaled)

    first = [(0, t) for t in range(tiles)]
    chunks = [first]
    if levels > 0:
        chunks = [first + [(1, t) for t in range(tiles)]]
    a, b = order
    later = [(level + 1, t) for level in range(1, levels - 2) for t in order]
    if levels > 2:
        later.append((levels - 1, a))
    chunks += [later[i : i + 3] for i in range(0, len(later), 3)]
    if levels > 2:
        chunks += [[(levels, a), (levels - 1, b)], [(levels, b)]]
    elif levels == 2:
        chunks += [[(levels, a)], [(levels, b)]]
    last = len(chunks) - 1

    for number, chunk in enumerate(chunks):
        for slot, t in chunk:
            if slot == 0:
                values_in(t, own2[t, WIDE:])
                continue
            level = slot - 1
            pltpu.make_async_remote_copy(
                own2.at[t], came.at[level, t],
                send_sem.at[4 + level * tiles + t], recv_sem.at[4 + level * tiles + t],
                device_id={"seq": partner(level)}, device_id_type=MESH,
            ).wait_recv()
            seen = mask[0, level] == 1
            piece = slot * tiles + t
            kb[level * tiles + t] = jnp.where(seen, came[level, t, :WIDE], own2[t, :WIDE])
            turned = came[level, t, WIDE:]
            values_in(piece, jnp.where(seen, turned, jnp.zeros_like(turned)))
            for group in range(2):
                vt[piece, group, HEAD_SIZE:] = jnp.where(
                    seen, jnp.ones((TOTALS, WIDE), bf16), jnp.zeros((TOTALS, WIDE), bf16)
                )

        def keys_of(slot, t):
            return own2[t, :WIDE] if slot == 0 else kb[(slot - 1) * tiles + t]

        def far_scores(h):
            keys = jnp.concatenate([keys_of(slot, t) for slot, t in chunk], axis=0)
            scores = dot(keys, queries_of(h))
            return [scores[i * WIDE : (i + 1) * WIDE] for i in range(len(chunk))]

        def far_weigh(h, parts):
            top = col_max(parts)
            fade = None
            if number > 0:
                before = jnp.concatenate([tops[t, h, 0:1] for t in range(tiles)], axis=1)
                top = jnp.maximum(before, top)
                fade = jnp.exp(before - top)
            if number < last:
                for t in range(tiles):
                    tops[t, h] = jnp.broadcast_to(top[:, t * WIDE : (t + 1) * WIDE], tops.shape[2:])
            return fade, [weight(part, top) for part in parts]

        def far_finish(h, fade, parts):
            acc = None
            if fade is not None:
                acc = jnp.concatenate([accs[t, h] for t in range(tiles)], axis=1) * fade
            for i in range(0, len(chunk), 2):
                lhs = both([slot * tiles + t for slot, t in chunk[i : i + 2]], vt, h // group_heads)
                term = dot(lhs, jnp.concatenate(parts[i : i + 2], axis=0))
                acc = term if acc is None else acc + term
            if number < last:
                for t in range(tiles):
                    accs[t, h] = acc[:, t * WIDE : (t + 1) * WIDE]
            else:
                put(h, shared(acc), slice(0, rows))

        staggered(heads, far_scores, far_weigh, far_finish)

    loads["wo2"].wait()
    out_ref[...] = (dot(att[...], wo2[...]) + hid[...].astype(f32)).astype(bf16)
    for level in swaps:
        for swap in level:
            swap.wait_send()
    for near in (True, False):

        @pl.when(has_right)
        def _():
            to_right(near).wait_send()

        @pl.when(has_left)
        def _():
            to_left(near).wait_send()


def shards(
    n, residual, layer_queries, layer_keyvals, head_window_extent, block_mask,
    first_out, second_query, second_keyval, second_out,
):
    levels = n.bit_length() - 1
    rows, width = residual.shape
    query_width = layer_queries.shape[1]
    kv_width = layer_keyvals.shape[1]
    tiles = rows // WIDE
    pieces = max(tiles + 4, (levels + 1) * tiles)
    bf16, f32 = jnp.bfloat16, jnp.float32
    stays = pl.BlockSpec(memory_space=pltpu.HBM)
    return pl.pallas_call(
        functools.partial(body, n, levels),
        name="two_layers",
        out_shape=pltpu.VMEM((rows, width), bf16),
        in_specs=[stays] * 9,
        out_specs=pl.BlockSpec(memory_space=pltpu.VMEM),
        scratch_shapes=[
            pltpu.VMEM((rows, query_width), bf16),
            pltpu.VMEM((rows, kv_width), bf16),
            pltpu.VMEM((rows, width), bf16),
            pltpu.VMEM(first_out.shape, bf16),
            pltpu.VMEM(second_query.shape, bf16),
            pltpu.VMEM(second_keyval.shape, bf16),
            pltpu.VMEM(second_out.shape, bf16),
            pltpu.VMEM((tiles, QUERY_HEADS, WIDE, WIDE), bf16),
            pltpu.VMEM((4, WIDE, kv_width), bf16),
            pltpu.VMEM((tiles, 2 * WIDE, WIDE), bf16),
            pltpu.VMEM((max(levels, 1), tiles, 2 * WIDE, WIDE), bf16),
            pltpu.VMEM((max(levels, 1) * tiles, WIDE, WIDE), bf16),
            pltpu.VMEM((pieces, 2, HEAD_SIZE + TOTALS, WIDE), bf16),
            pltpu.VMEM((tiles, QUERY_HEADS, 8, WIDE), f32),
            pltpu.VMEM((tiles, QUERY_HEADS, HEAD_SIZE + TOTALS, WIDE), f32),
            pltpu.VMEM((rows, query_width), bf16),
            pltpu.VMEM((rows, width), bf16),
            pltpu.VMEM((rows, width), bf16),
            pltpu.SMEM(head_window_extent.shape, jnp.int32),
            pltpu.SMEM(block_mask.shape, jnp.int32),
            pltpu.SemaphoreType.DMA((9,)),
            pltpu.SemaphoreType.DMA((4 + levels * tiles,)),
            pltpu.SemaphoreType.DMA((4 + levels * tiles,)),
            pltpu.SemaphoreType.REGULAR((max(levels - 1, 1),)),
        ],
        compiler_params=pltpu.CompilerParams(
            collective_id=0, has_side_effects=True
        ),
    )(
        layer_queries, layer_keyvals, residual, head_window_extent, block_mask,
        first_out, second_query, second_keyval, second_out,
    )


def solution(mesh):
    placed = (
        P(("groups", "seq"), None),
        P(("groups", "seq"), None),
        P(("groups", "seq"), None),
        P(),
        P("seq", None),
        P(),
        P(),
        P(),
        P(),
    )
    return jax.shard_map(
        functools.partial(shards, mesh.shape["seq"]),
        mesh=mesh, in_specs=placed, out_specs=P(("groups", "seq"), None), check_vma=False,
    )
```

```python
import functools

import jax
import jax.numpy as jnp
from jax import lax
from jax.experimental import pallas as pl
from jax.experimental.pallas import tpu as pltpu
from jax.sharding import PartitionSpec as P

QUERY_HEADS = 8
HEAD_SIZE = 64
WIDE = 2 * HEAD_SIZE
MESH = pl.DeviceIdType.MESH
HIDE = -1e30
TOTALS = 16


def dot(a, b):
    return jnp.dot(a, b, preferred_element_type=jnp.float32)


def col_max(parts):
    top = jnp.max(parts[0], axis=0, keepdims=True)
    for part in parts[1:]:
        top = jnp.maximum(top, jnp.max(part, axis=0, keepdims=True))
    return top


def weight(scores, top):
    return jnp.exp((scores - top).astype(jnp.bfloat16))


def staggered(steps, scores, weigh, finish):
    ready, weighed = {}, {}
    count = len(steps)
    for at in range(count + 2):
        if at < count:
            ready[at] = scores(steps[at])
        if 0 <= at - 1 < count:
            weighed[at - 1] = weigh(steps[at - 1], ready.pop(at - 1))
        if 0 <= at - 2 < count:
            finish(steps[at - 2], *weighed.pop(at - 2))


def shared(acc):
    return acc[:HEAD_SIZE] * (1.0 / acc[HEAD_SIZE : HEAD_SIZE + 1])


def body(
    n, levels,
    q_hbm, kv_hbm, res_hbm, extent_hbm, mask_hbm, wo1_hbm, wq2_hbm, wkv2_hbm, wo2_hbm,
    att, hid, wo2,
    q, kv, res, wo1, wq2, wkv2, qx, halo, own2, came, kb, vt, tops, accs, norm,
    extent, mask, local_sem, send_sem, recv_sem, enter_sem,
):
    rows = q.shape[0]
    tiles = rows // WIDE
    pairs = q.shape[1] // WIDE
    group_heads = pairs
    heads = list(range(2 * pairs))
    bf16, f32 = jnp.bfloat16, jnp.float32
    scaled = bf16(HEAD_SIZE ** (-0.5))
    me = lax.axis_index("seq")
    loads = {
        name: pltpu.make_async_copy(src, dst, local_sem.at[i])
        for i, (name, src, dst) in enumerate(
            (
                ("kv", kv_hbm, kv),
                ("q", q_hbm, q),
                ("extent", extent_hbm, extent),
                ("mask", mask_hbm, mask),
                ("wo1", wo1_hbm, wo1),
                ("res", res_hbm, res),
                ("wkv2", wkv2_hbm, wkv2),
                ("wq2", wq2_hbm, wq2),
                ("wo2", wo2_hbm, wo2),
            )
        )
    }
    barrier = pltpu.get_barrier_semaphore()
    has_left, has_right = me > 0, me < n - 1

    def partner(level):
        bit = lax.rem(lax.div(me, 1 << level), 2)
        return me + (1 << level) * (1 - 2 * bit)

    def tell(sem, reach):
        @pl.when(me >= reach)
        def _():
            pl.semaphore_signal(sem, inc=1, device_id={"seq": me - reach}, device_id_type=MESH)

        @pl.when(me < n - reach)
        def _():
            pl.semaphore_signal(sem, inc=1, device_id={"seq": me + reach}, device_id_type=MESH)

    def told(sem, reach):
        pl.semaphore_wait(sem, (me >= reach).astype(jnp.int32) + (me < n - reach).astype(jnp.int32))

    tell(barrier, 1)
    for load in loads.values():
        load.start()

    def to_right(near):
        slot = 1 if near else 0
        return pltpu.make_async_remote_copy(
            kv_hbm.at[pl.ds(slot * WIDE, WIDE)], halo.at[slot], send_sem.at[slot], recv_sem.at[slot],
            device_id={"seq": me + 1}, device_id_type=MESH,
        )

    def to_left(near):
        slot = 2 if near else 3
        return pltpu.make_async_remote_copy(
            kv_hbm.at[pl.ds((slot - 2) * WIDE, WIDE)], halo.at[slot], send_sem.at[slot], recv_sem.at[slot],
            device_id={"seq": me - 1}, device_id_type=MESH,
        )

    told(barrier, 1)
    def send_halo(near):
        @pl.when(has_right)
        def _():
            to_right(near).start()

        @pl.when(has_left)
        def _():
            to_left(near).start()

    send_halo(True)

    stages = max(levels - 1, 0)

    def go_on(stage):
        if stage < stages:
            told(enter_sem.at[stage], 1 << stage)
            if stage + 1 < stages:
                tell(enter_sem.at[stage + 1], 1 << (stage + 1))

    if stages:
        tell(enter_sem.at[0], 1)

    for piece in range(vt.shape[0]):
        for group in range(2):
            vt[piece, group, HEAD_SIZE:] = jnp.ones((TOTALS, WIDE), bf16)

    @pl.when(jnp.logical_not(has_left))
    def _():
        halo[0:2] = jnp.zeros((2, *halo.shape[1:]), bf16)

    @pl.when(jnp.logical_not(has_right))
    def _():
        halo[2:4] = jnp.zeros((2, *halo.shape[1:]), bf16)

    def values_in(piece, turned):
        for group in range(2):
            vt[piece, group, :HEAD_SIZE] = turned[group * HEAD_SIZE : (group + 1) * HEAD_SIZE]

    def spread_queries(block):
        for pair in range(pairs):
            for t in range(tiles):
                turned = block[t * WIDE : (t + 1) * WIDE, pair * WIDE : (pair + 1) * WIDE].T
                for h in (2 * pair, 2 * pair + 1):
                    group = h // group_heads
                    start = group * HEAD_SIZE
                    qx[t, h, start : start + HEAD_SIZE] = turned[h % 2 * HEAD_SIZE : (h % 2 + 1) * HEAD_SIZE]

    for h in heads:
        start = (1 - h // group_heads) * HEAD_SIZE
        qx[:, h, start : start + HEAD_SIZE] = jnp.zeros((tiles, HEAD_SIZE, WIDE), bf16)

    def queries_of(h):
        return jnp.concatenate([qx[t, h] for t in range(tiles)], axis=1)

    loads["kv"].wait()
    for t in range(tiles):
        values_in(t, kv[t * WIDE : (t + 1) * WIDE, WIDE:].T)
    loads["q"].wait()
    loads["extent"].wait()
    loads["mask"].wait()
    spread_queries(q[...] * scaled)
    send_halo(False)

    def both(pieces, ref, group):
        return jnp.concatenate([ref[p, group] for p in pieces], axis=1)

    key = lax.broadcasted_iota(jnp.int32, (rows, rows), 0)
    query = lax.broadcasted_iota(jnp.int32, (rows, rows), 1)
    apart = jnp.abs(key - query)

    def own_scores(h):
        return (dot(kv[:, :WIDE], queries_of(h)),)

    def own_weigh(h, parts):
        scores = jnp.where(apart <= extent[h], parts[0], HIDE)
        top = col_max([scores])
        for t in range(tiles):
            tops[t, h] = jnp.broadcast_to(top[:, t * WIDE : (t + 1) * WIDE], tops.shape[2:])
        return (weight(scores, top),)

    def own_finish(h, shares):
        acc = dot(both(range(tiles), vt, h // group_heads), shares)
        for t in range(tiles):
            accs[t, h] = acc[:, t * WIDE : (t + 1) * WIDE]

    half = len(heads) // 2
    staggered(heads[:half], own_scores, own_weigh, own_finish)
    go_on(0)
    staggered(heads[half:], own_scores, own_weigh, own_finish)
    go_on(1)

    @pl.when(has_left)
    def _():
        to_right(True).wait_recv()

    @pl.when(has_right)
    def _():
        to_left(True).wait_recv()

    for piece in (1, 2):
        values_in(tiles + piece, halo[piece, :, WIDE:].T)

    parity = lax.rem(me, 2)
    order = (1 - parity, parity)
    far = 4 * n * rows
    left_off = jnp.where(has_left, 0, far)
    right_off = jnp.where(has_right, 0, far)
    delta = (
        lax.broadcasted_iota(jnp.int32, (WIDE, WIDE), 1)
        - lax.broadcasted_iota(jnp.int32, (WIDE, WIDE), 0)
    )
    swaps = [
        [
            pltpu.make_async_remote_copy(
                own2.at[t], came.at[level, t],
                send_sem.at[4 + level * tiles + t], recv_sem.at[4 + level * tiles + t],
                device_id={"seq": partner(level)}, device_id_type=MESH,
            )
            for t in order
        ]
        for level in range(levels)
    ]
    halves = []

    def put(h, share, where_to):
        halves.append(share)
        if h % 2:
            pair = jnp.concatenate(halves, axis=0).astype(bf16)
            att[where_to, h // 2 * WIDE : (h // 2 + 1) * WIDE] = pair.T
            halves.clear()

    for name in ("wo1", "res", "wkv2"):
        loads[name].wait()
    for step, t in enumerate(order):
        here = pl.ds(pl.multiple_of(t * WIDE, WIDE), WIDE)
        at_left = t == 0

        @pl.when(jnp.logical_and(at_left, has_left))
        def _():
            to_right(False).wait_recv()

        @pl.when(jnp.logical_and(jnp.logical_not(at_left), has_right))
        def _():
            to_left(False).wait_recv()

        far_piece = 3 * t
        values_in(tiles + far_piece, halo[far_piece, :, WIDE:].T)
        sign = 1 - 2 * t
        off_mid = jnp.where(at_left, left_off, right_off)
        middle = delta * sign

        def twice(ref, h):
            return jnp.concatenate([ref[t, h], ref[t, h + 1]], axis=1)

        def side_scores(h):
            keys = jnp.concatenate([halo[t + i, :, :WIDE] for i in range(3)], axis=0)
            scores = dot(keys, twice(qx, h))
            return [scores[i * WIDE : (i + 1) * WIDE] for i in range(3)]

        def side_weigh(h, parts):
            kept = []
            for k in range(2):
                reach = extent[h + k]
                a, b, c = (part[:, k * WIDE : (k + 1) * WIDE] for part in parts)
                kept.append((
                    jnp.where(delta <= reach - rows - left_off, a, HIDE),
                    jnp.where(middle <= reach - WIDE - off_mid, b, HIDE),
                    jnp.where(delta >= rows + right_off - reach, c, HIDE),
                ))
            shares, fades = [], []
            for k in range(2):
                before = tops[t, h + k, 0:1]
                top = jnp.maximum(before, col_max(kept[k]))
                fades.append(jnp.exp(before - top))
                shares.append(jnp.concatenate([weight(x, top) for x in kept[k]], axis=0))
            return jnp.concatenate(fades, axis=1), jnp.concatenate(shares, axis=1)

        def side_finish(h, fade, shares):
            lhs = both([tiles + t + i for i in range(3)], vt, h // group_heads)
            acc = twice(accs, h) * fade + dot(lhs, shares)
            for k in range(2):
                put(h + k, shared(acc[:, k * WIDE : (k + 1) * WIDE]), here)

        staggered(heads[::2], side_scores, side_weigh, side_finish)

        hidden = (dot(att[here], wo1[...]) + res[here].astype(f32)).astype(bf16)
        hid[here] = hidden
        values = hidden.astype(f32)
        scale = lax.rsqrt(jnp.mean(values * values, axis=-1, keepdims=True) + 1e-05)
        normed = (values * scale).astype(bf16)
        norm[here] = normed
        keyvals = dot(normed, wkv2[...]).astype(bf16)
        own2[t, :WIDE] = keyvals[:, :WIDE]
        own2[t, WIDE:] = keyvals[:, WIDE:].T
        if step == 0:
            for stage in range(2, stages):
                go_on(stage)
        for swap in reversed(swaps):
            swap[step].start()

    loads["wq2"].wait()
    spread_queries(dot(norm[...], wq2[...]).astype(bf16) * scaled)

    first = [(0, t) for t in range(tiles)]
    chunks = [first]
    if levels > 0:
        chunks = [first + [(1, t) for t in range(tiles)]]
    a, b = order
    later = [(level + 1, t) for level in range(1, levels - 2) for t in order]
    if levels > 2:
        later.append((levels - 1, a))
    chunks += [later[i : i + 3] for i in range(0, len(later), 3)]
    if levels > 2:
        chunks += [[(levels, a), (levels - 1, b)], [(levels, b)]]
    elif levels == 2:
        chunks += [[(levels, a)], [(levels, b)]]
    last = len(chunks) - 1

    for number, chunk in enumerate(chunks):
        for slot, t in chunk:
            if slot == 0:
                values_in(t, own2[t, WIDE:])
                continue
            level = slot - 1
            pltpu.make_async_remote_copy(
                own2.at[t], came.at[level, t],
                send_sem.at[4 + level * tiles + t], recv_sem.at[4 + level * tiles + t],
                device_id={"seq": partner(level)}, device_id_type=MESH,
            ).wait_recv()
            seen = mask[0, level] == 1
            piece = slot * tiles + t
            kb[level * tiles + t] = jnp.where(seen, came[level, t, :WIDE], own2[t, :WIDE])
            turned = came[level, t, WIDE:]
            values_in(piece, jnp.where(seen, turned, jnp.zeros_like(turned)))
            for group in range(2):
                vt[piece, group, HEAD_SIZE:] = jnp.where(
                    seen, jnp.ones((TOTALS, WIDE), bf16), jnp.zeros((TOTALS, WIDE), bf16)
                )

        def keys_of(slot, t):
            return own2[t, :WIDE] if slot == 0 else kb[(slot - 1) * tiles + t]

        def far_scores(h):
            keys = jnp.concatenate([keys_of(slot, t) for slot, t in chunk], axis=0)
            scores = dot(keys, queries_of(h))
            return [scores[i * WIDE : (i + 1) * WIDE] for i in range(len(chunk))]

        def far_weigh(h, parts):
            top = col_max(parts)
            fade = None
            if number > 0:
                before = jnp.concatenate([tops[t, h, 0:1] for t in range(tiles)], axis=1)
                top = jnp.maximum(before, top)
                fade = jnp.exp(before - top)
            if number < last:
                for t in range(tiles):
                    tops[t, h] = jnp.broadcast_to(top[:, t * WIDE : (t + 1) * WIDE], tops.shape[2:])
            return fade, [weight(part, top) for part in parts]

        def far_finish(h, fade, parts):
            acc = None
            if fade is not None:
                acc = jnp.concatenate([accs[t, h] for t in range(tiles)], axis=1) * fade
            for i in range(0, len(chunk), 2):
                lhs = both([slot * tiles + t for slot, t in chunk[i : i + 2]], vt, h // group_heads)
                term = dot(lhs, jnp.concatenate(parts[i : i + 2], axis=0))
                acc = term if acc is None else acc + term
            if number < last:
                for t in range(tiles):
                    accs[t, h] = acc[:, t * WIDE : (t + 1) * WIDE]
            else:
                put(h, shared(acc), slice(0, rows))

        staggered(heads, far_scores, far_weigh, far_finish)

    loads["wo2"].wait()
    for level in swaps:
        for swap in level:
            swap.wait_send()
    for near in (True, False):

        @pl.when(has_right)
        def _():
            to_right(near).wait_send()

        @pl.when(has_left)
        def _():
            to_left(near).wait_send()


def project(att, hid, weight_ref, out_hbm, out, sem):
    width = out.shape[1]
    step = min(width, 4 * WIDE)
    copies = []
    for start in range(0, width, step):
        here = pl.ds(start, step)
        total = dot(att[...], weight_ref[:, here]) + hid[:, here].astype(jnp.float32)
        out[:, here] = total.astype(out.dtype)
        copies.append(pltpu.make_async_copy(out.at[:, here], out_hbm.at[:, here], sem.at[len(copies)]))
        copies[-1].start()
    for copy in copies:
        copy.wait()


def shards(
    n, residual, layer_queries, layer_keyvals, head_window_extent, block_mask,
    first_out, second_query, second_keyval, second_out,
):
    levels = n.bit_length() - 1
    rows, width = residual.shape
    query_width = layer_queries.shape[1]
    kv_width = layer_keyvals.shape[1]
    tiles = rows // WIDE
    pieces = max(tiles + 4, (levels + 1) * tiles)
    bf16, f32 = jnp.bfloat16, jnp.float32
    stays = pl.BlockSpec(memory_space=pltpu.HBM)
    held = pl.BlockSpec(memory_space=pltpu.VMEM)
    att, hidden, weights = pl.pallas_call(
        functools.partial(body, n, levels),
        name="two_layers",
        out_shape=(
            pltpu.VMEM((rows, query_width), bf16),
            pltpu.VMEM((rows, width), bf16),
            pltpu.VMEM(second_out.shape, bf16),
        ),
        in_specs=[stays] * 9,
        out_specs=(held, held, held),
        scratch_shapes=[
            pltpu.VMEM((rows, query_width), bf16),
            pltpu.VMEM((rows, kv_width), bf16),
            pltpu.VMEM((rows, width), bf16),
            pltpu.VMEM(first_out.shape, bf16),
            pltpu.VMEM(second_query.shape, bf16),
            pltpu.VMEM(second_keyval.shape, bf16),
            pltpu.VMEM((tiles, QUERY_HEADS, WIDE, WIDE), bf16),
            pltpu.VMEM((4, WIDE, kv_width), bf16),
            pltpu.VMEM((tiles, 2 * WIDE, WIDE), bf16),
            pltpu.VMEM((max(levels, 1), tiles, 2 * WIDE, WIDE), bf16),
            pltpu.VMEM((max(levels, 1) * tiles, WIDE, WIDE), bf16),
            pltpu.VMEM((pieces, 2, HEAD_SIZE + TOTALS, WIDE), bf16),
            pltpu.VMEM((tiles, QUERY_HEADS, 8, WIDE), f32),
            pltpu.VMEM((tiles, QUERY_HEADS, HEAD_SIZE + TOTALS, WIDE), f32),
            pltpu.VMEM((rows, width), bf16),
            pltpu.SMEM(head_window_extent.shape, jnp.int32),
            pltpu.SMEM(block_mask.shape, jnp.int32),
            pltpu.SemaphoreType.DMA((9,)),
            pltpu.SemaphoreType.DMA((4 + levels * tiles,)),
            pltpu.SemaphoreType.DMA((4 + levels * tiles,)),
            pltpu.SemaphoreType.REGULAR((max(levels - 1, 1),)),
        ],
        compiler_params=pltpu.CompilerParams(
            collective_id=0, has_side_effects=True
        ),
    )(
        layer_queries, layer_keyvals, residual, head_window_extent, block_mask,
        first_out, second_query, second_keyval, second_out,
    )
    return pl.pallas_call(
        project,
        name="project",
        out_shape=jax.ShapeDtypeStruct((rows, width), bf16),
        in_specs=[held] * 3,
        out_specs=pl.BlockSpec(memory_space=pl.ANY),
        scratch_shapes=[
            pltpu.VMEM((rows, width), bf16),
            pltpu.SemaphoreType.DMA((max(1, width // (4 * WIDE)),)),
        ],
        compiler_params=pltpu.CompilerParams(vmem_limit_bytes=16 * 2**20),
    )(*(pltpu.with_memory_space_constraint(x, pltpu.VMEM) for x in (att, hidden, weights)))


def solution(mesh):
    placed = (
        P(("groups", "seq"), None),
        P(("groups", "seq"), None),
        P(("groups", "seq"), None),
        P(),
        P("seq", None),
        P(),
        P(),
        P(),
        P(),
    )
    return jax.shard_map(
        functools.partial(shards, mesh.shape["seq"]),
        mesh=mesh, in_specs=placed, out_specs=P(("groups", "seq"), None), check_vma=False,
    )
```

```python
import functools

import jax
import jax.numpy as jnp
from jax import lax
from jax.experimental import pallas as pl
from jax.experimental.pallas import tpu as pltpu
from jax.sharding import PartitionSpec as P

QUERY_HEADS = 8
HEAD_SIZE = 64
WIDE = 2 * HEAD_SIZE
MESH = pl.DeviceIdType.MESH
HIDE = -1e30
TOTALS = 16


def dot(a, b):
    return jnp.dot(a, b, preferred_element_type=jnp.float32)


def col_max(parts):
    top = jnp.max(parts[0], axis=0, keepdims=True)
    for part in parts[1:]:
        top = jnp.maximum(top, jnp.max(part, axis=0, keepdims=True))
    return top


def weight(scores, top):
    return jnp.exp((scores - top).astype(jnp.bfloat16))


def staggered(steps, scores, weigh, finish):
    ready, weighed = {}, {}
    count = len(steps)
    for at in range(count + 2):
        if at < count:
            ready[at] = scores(steps[at])
        if 0 <= at - 1 < count:
            weighed[at - 1] = weigh(steps[at - 1], ready.pop(at - 1))
        if 0 <= at - 2 < count:
            finish(steps[at - 2], *weighed.pop(at - 2))


def shared(acc):
    return acc[:HEAD_SIZE] * (1.0 / acc[HEAD_SIZE : HEAD_SIZE + 1])


def body(
    n, levels,
    q_hbm, kv_hbm, res_hbm, extent_hbm, mask_hbm, wo1_hbm, wq2_hbm, wkv2_hbm, wo2_hbm,
    att, hid, wo2,
    q, kv, res, wo1, wq2, wkv2, qx, halo, own2, came, kb, vt, tops, accs, norm,
    extent, mask, local_sem, send_sem, recv_sem, enter_sem,
):
    rows = q.shape[0]
    tiles = rows // WIDE
    pairs = q.shape[1] // WIDE
    group_heads = pairs
    heads = list(range(2 * pairs))
    bf16, f32 = jnp.bfloat16, jnp.float32
    scaled = bf16(HEAD_SIZE ** (-0.5))
    me = lax.axis_index("seq")
    loads = {
        name: pltpu.make_async_copy(src, dst, local_sem.at[i])
        for i, (name, src, dst) in enumerate(
            (
                ("kv", kv_hbm, kv),
                ("q", q_hbm, q),
                ("extent", extent_hbm, extent),
                ("mask", mask_hbm, mask),
                ("wo1", wo1_hbm, wo1),
                ("res", res_hbm, res),
                ("wkv2", wkv2_hbm, wkv2),
                ("wq2", wq2_hbm, wq2),
                ("wo2", wo2_hbm, wo2),
            )
        )
    }
    barrier = pltpu.get_barrier_semaphore()
    has_left, has_right = me > 0, me < n - 1

    def partner(level):
        bit = lax.rem(lax.div(me, 1 << level), 2)
        return me + (1 << level) * (1 - 2 * bit)

    def tell(sem, reach):
        @pl.when(me >= reach)
        def _():
            pl.semaphore_signal(sem, inc=1, device_id={"seq": me - reach}, device_id_type=MESH)

        @pl.when(me < n - reach)
        def _():
            pl.semaphore_signal(sem, inc=1, device_id={"seq": me + reach}, device_id_type=MESH)

    def told(sem, reach):
        pl.semaphore_wait(sem, (me >= reach).astype(jnp.int32) + (me < n - reach).astype(jnp.int32))

    tell(barrier, 1)
    for load in loads.values():
        load.start()

    def to_right(near):
        slot = 1 if near else 0
        return pltpu.make_async_remote_copy(
            kv_hbm.at[pl.ds(slot * WIDE, WIDE)], halo.at[slot], send_sem.at[0], recv_sem.at[slot],
            device_id={"seq": me + 1}, device_id_type=MESH,
        )

    def to_left(near):
        slot = 2 if near else 3
        return pltpu.make_async_remote_copy(
            kv_hbm.at[pl.ds((slot - 2) * WIDE, WIDE)], halo.at[slot], send_sem.at[1], recv_sem.at[slot],
            device_id={"seq": me - 1}, device_id_type=MESH,
        )

    told(barrier, 1)
    def send_halo(near):
        @pl.when(has_right)
        def _():
            to_right(near).start()

        @pl.when(has_left)
        def _():
            to_left(near).start()

    send_halo(True)

    stages = max(levels - 1, 0)

    def go_on(stage):
        if stage < stages:
            told(enter_sem.at[stage], 1 << stage)
            if stage + 1 < stages:
                tell(enter_sem.at[stage + 1], 1 << (stage + 1))

    if stages:
        tell(enter_sem.at[0], 1)

    for piece in range(vt.shape[0]):
        for group in range(2):
            vt[piece, group, HEAD_SIZE:] = jnp.ones((TOTALS, WIDE), bf16)

    @pl.when(jnp.logical_not(has_left))
    def _():
        halo[0:2] = jnp.zeros((2, *halo.shape[1:]), bf16)

    @pl.when(jnp.logical_not(has_right))
    def _():
        halo[2:4] = jnp.zeros((2, *halo.shape[1:]), bf16)

    def values_in(piece, turned):
        for group in range(2):
            vt[piece, group, :HEAD_SIZE] = turned[group * HEAD_SIZE : (group + 1) * HEAD_SIZE]

    def spread_queries(block):
        for pair in range(pairs):
            for t in range(tiles):
                turned = block[t * WIDE : (t + 1) * WIDE, pair * WIDE : (pair + 1) * WIDE].T
                for h in (2 * pair, 2 * pair + 1):
                    group = h // group_heads
                    start = group * HEAD_SIZE
                    qx[t, h, start : start + HEAD_SIZE] = turned[h % 2 * HEAD_SIZE : (h % 2 + 1) * HEAD_SIZE]

    for h in heads:
        start = (1 - h // group_heads) * HEAD_SIZE
        qx[:, h, start : start + HEAD_SIZE] = jnp.zeros((tiles, HEAD_SIZE, WIDE), bf16)

    def queries_of(h):
        return jnp.concatenate([qx[t, h] for t in range(tiles)], axis=1)

    loads["kv"].wait()
    for t in range(tiles):
        values_in(t, kv[t * WIDE : (t + 1) * WIDE, WIDE:].T)
    loads["q"].wait()
    loads["extent"].wait()
    loads["mask"].wait()
    spread_queries(q[...] * scaled)
    send_halo(False)

    def both(pieces, ref, group):
        return jnp.concatenate([ref[p, group] for p in pieces], axis=1)

    key = lax.broadcasted_iota(jnp.int32, (rows, rows), 0)
    query = lax.broadcasted_iota(jnp.int32, (rows, rows), 1)
    apart = jnp.abs(key - query)

    def own_scores(h):
        return (dot(kv[:, :WIDE], queries_of(h)),)

    def own_weigh(h, parts):
        scores = jnp.where(apart <= extent[h], parts[0], HIDE)
        top = col_max([scores])
        for t in range(tiles):
            tops[t, h] = jnp.broadcast_to(top[:, t * WIDE : (t + 1) * WIDE], tops.shape[2:])
        return (weight(scores, top),)

    def own_finish(h, shares):
        acc = dot(both(range(tiles), vt, h // group_heads), shares)
        for t in range(tiles):
            accs[t, h] = acc[:, t * WIDE : (t + 1) * WIDE]

    half = len(heads) // 2
    staggered(heads[:half], own_scores, own_weigh, own_finish)
    go_on(0)
    staggered(heads[half:], own_scores, own_weigh, own_finish)
    go_on(1)

    @pl.when(has_left)
    def _():
        to_right(True).wait_recv()

    @pl.when(has_right)
    def _():
        to_left(True).wait_recv()

    for piece in (1, 2):
        values_in(tiles + piece, halo[piece, :, WIDE:].T)

    parity = lax.rem(me, 2)
    order = (1 - parity, parity)
    far = 4 * n * rows
    left_off = jnp.where(has_left, 0, far)
    right_off = jnp.where(has_right, 0, far)
    delta = (
        lax.broadcasted_iota(jnp.int32, (WIDE, WIDE), 1)
        - lax.broadcasted_iota(jnp.int32, (WIDE, WIDE), 0)
    )
    swaps = [
        [
            pltpu.make_async_remote_copy(
                own2.at[t], came.at[level, t],
                send_sem.at[2], recv_sem.at[4 + level * tiles + t],
                device_id={"seq": partner(level)}, device_id_type=MESH,
            )
            for t in order
        ]
        for level in range(levels)
    ]
    halves = []

    def put(h, share, where_to):
        halves.append(share)
        if h % 2:
            pair = jnp.concatenate(halves, axis=0).astype(bf16)
            att[where_to, h // 2 * WIDE : (h // 2 + 1) * WIDE] = pair.T
            halves.clear()

    for name in ("wo1", "res", "wkv2"):
        loads[name].wait()
    for step, t in enumerate(order):
        here = pl.ds(pl.multiple_of(t * WIDE, WIDE), WIDE)
        at_left = t == 0

        @pl.when(jnp.logical_and(at_left, has_left))
        def _():
            to_right(False).wait_recv()

        @pl.when(jnp.logical_and(jnp.logical_not(at_left), has_right))
        def _():
            to_left(False).wait_recv()

        far_piece = 3 * t
        values_in(tiles + far_piece, halo[far_piece, :, WIDE:].T)
        sign = 1 - 2 * t
        off_mid = jnp.where(at_left, left_off, right_off)
        middle = delta * sign

        def twice(ref, h):
            return jnp.concatenate([ref[t, h], ref[t, h + 1]], axis=1)

        def side_scores(h):
            keys = jnp.concatenate([halo[t + i, :, :WIDE] for i in range(3)], axis=0)
            scores = dot(keys, twice(qx, h))
            return [scores[i * WIDE : (i + 1) * WIDE] for i in range(3)]

        def side_weigh(h, parts):
            kept = []
            for k in range(2):
                reach = extent[h + k]
                a, b, c = (part[:, k * WIDE : (k + 1) * WIDE] for part in parts)
                kept.append((
                    jnp.where(delta <= reach - rows - left_off, a, HIDE),
                    jnp.where(middle <= reach - WIDE - off_mid, b, HIDE),
                    jnp.where(delta >= rows + right_off - reach, c, HIDE),
                ))
            shares, fades = [], []
            for k in range(2):
                before = tops[t, h + k, 0:1]
                top = jnp.maximum(before, col_max(kept[k]))
                fades.append(jnp.exp(before - top))
                shares.append(jnp.concatenate([weight(x, top) for x in kept[k]], axis=0))
            return jnp.concatenate(fades, axis=1), jnp.concatenate(shares, axis=1)

        def side_finish(h, fade, shares):
            lhs = both([tiles + t + i for i in range(3)], vt, h // group_heads)
            acc = twice(accs, h) * fade + dot(lhs, shares)
            for k in range(2):
                put(h + k, shared(acc[:, k * WIDE : (k + 1) * WIDE]), here)

        staggered(heads[::2], side_scores, side_weigh, side_finish)

        hidden = (dot(att[here], wo1[...]) + res[here].astype(f32)).astype(bf16)
        hid[here] = hidden
        values = hidden.astype(f32)
        scale = lax.rsqrt(jnp.mean(values * values, axis=-1, keepdims=True) + 1e-05)
        normed = (values * scale).astype(bf16)
        norm[here] = normed
        keyvals = dot(normed, wkv2[...]).astype(bf16)
        own2[t, :WIDE] = keyvals[:, :WIDE]
        own2[t, WIDE:] = keyvals[:, WIDE:].T
        if step == 0:
            for stage in range(2, stages):
                go_on(stage)
        for swap in reversed(swaps):
            swap[step].start()

    loads["wq2"].wait()
    spread_queries(dot(norm[...], wq2[...]).astype(bf16) * scaled)

    first = [(0, t) for t in range(tiles)]
    chunks = [first]
    if levels > 0:
        chunks = [first + [(1, t) for t in range(tiles)]]
    a, b = order
    later = [(level + 1, t) for level in range(1, levels - 2) for t in order]
    if levels > 2:
        later.append((levels - 1, a))
    chunks += [later[i : i + 3] for i in range(0, len(later), 3)]
    if levels > 2:
        chunks += [[(levels, a), (levels - 1, b)], [(levels, b)]]
    elif levels == 2:
        chunks += [[(levels, a)], [(levels, b)]]
    last = len(chunks) - 1

    for number, chunk in enumerate(chunks):
        for slot, t in chunk:
            if slot == 0:
                values_in(t, own2[t, WIDE:])
                continue
            level = slot - 1
            pltpu.make_async_remote_copy(
                own2.at[t], came.at[level, t],
                send_sem.at[2], recv_sem.at[4 + level * tiles + t],
                device_id={"seq": partner(level)}, device_id_type=MESH,
            ).wait_recv()
            seen = mask[0, level] == 1
            piece = slot * tiles + t
            kb[level * tiles + t] = jnp.where(seen, came[level, t, :WIDE], own2[t, :WIDE])
            turned = came[level, t, WIDE:]
            values_in(piece, jnp.where(seen, turned, jnp.zeros_like(turned)))
            for group in range(2):
                vt[piece, group, HEAD_SIZE:] = jnp.where(
                    seen, jnp.ones((TOTALS, WIDE), bf16), jnp.zeros((TOTALS, WIDE), bf16)
                )

        def keys_of(slot, t):
            return own2[t, :WIDE] if slot == 0 else kb[(slot - 1) * tiles + t]

        def far_scores(h):
            keys = jnp.concatenate([keys_of(slot, t) for slot, t in chunk], axis=0)
            scores = dot(keys, queries_of(h))
            return [scores[i * WIDE : (i + 1) * WIDE] for i in range(len(chunk))]

        def far_weigh(h, parts):
            top = col_max(parts)
            fade = None
            if number > 0:
                before = jnp.concatenate([tops[t, h, 0:1] for t in range(tiles)], axis=1)
                top = jnp.maximum(before, top)
                fade = jnp.exp(before - top)
            if number < last:
                for t in range(tiles):
                    tops[t, h] = jnp.broadcast_to(top[:, t * WIDE : (t + 1) * WIDE], tops.shape[2:])
            return fade, [weight(part, top) for part in parts]

        def far_finish(h, fade, parts):
            acc = None
            if fade is not None:
                acc = jnp.concatenate([accs[t, h] for t in range(tiles)], axis=1) * fade
            for i in range(0, len(chunk), 2):
                lhs = both([slot * tiles + t for slot, t in chunk[i : i + 2]], vt, h // group_heads)
                term = dot(lhs, jnp.concatenate(parts[i : i + 2], axis=0))
                acc = term if acc is None else acc + term
            if number < last:
                for t in range(tiles):
                    accs[t, h] = acc[:, t * WIDE : (t + 1) * WIDE]
            else:
                put(h, shared(acc), slice(0, rows))

        staggered(heads, far_scores, far_weigh, far_finish)

    loads["wo2"].wait()
    def sent(sem, whole):
        pltpu.make_async_remote_copy(
            whole, whole, send_sem.at[sem], recv_sem.at[0],
            device_id={"seq": partner(0)}, device_id_type=MESH,
        ).wait_send()

    if levels:
        sent(2, came)

    @pl.when(has_right)
    def _():
        sent(0, halo.at[pl.ds(0, 2)])

    @pl.when(has_left)
    def _():
        sent(1, halo.at[pl.ds(0, 2)])


def project(att, hid, weight_ref, out_hbm, out, sem):
    width = out.shape[1]
    step = min(width, 4 * WIDE)
    copies = []
    for start in range(0, width, step):
        here = pl.ds(start, step)
        total = dot(att[...], weight_ref[:, here]) + hid[:, here].astype(jnp.float32)
        out[:, here] = total.astype(out.dtype)
        copies.append(pltpu.make_async_copy(out.at[:, here], out_hbm.at[:, here], sem.at[len(copies)]))
        copies[-1].start()
    for copy in copies:
        copy.wait()


def shards(
    n, residual, layer_queries, layer_keyvals, head_window_extent, block_mask,
    first_out, second_query, second_keyval, second_out,
):
    levels = n.bit_length() - 1
    rows, width = residual.shape
    query_width = layer_queries.shape[1]
    kv_width = layer_keyvals.shape[1]
    tiles = rows // WIDE
    pieces = max(tiles + 4, (levels + 1) * tiles)
    bf16, f32 = jnp.bfloat16, jnp.float32
    stays = pl.BlockSpec(memory_space=pltpu.HBM)
    held = pl.BlockSpec(memory_space=pltpu.VMEM)
    att, hidden, weights = pl.pallas_call(
        functools.partial(body, n, levels),
        name="two_layers",
        out_shape=(
            pltpu.VMEM((rows, query_width), bf16),
            pltpu.VMEM((rows, width), bf16),
            pltpu.VMEM(second_out.shape, bf16),
        ),
        in_specs=[stays] * 9,
        out_specs=(held, held, held),
        scratch_shapes=[
            pltpu.VMEM((rows, query_width), bf16),
            pltpu.VMEM((rows, kv_width), bf16),
            pltpu.VMEM((rows, width), bf16),
            pltpu.VMEM(first_out.shape, bf16),
            pltpu.VMEM(second_query.shape, bf16),
            pltpu.VMEM(second_keyval.shape, bf16),
            pltpu.VMEM((tiles, QUERY_HEADS, WIDE, WIDE), bf16),
            pltpu.VMEM((4, WIDE, kv_width), bf16),
            pltpu.VMEM((tiles, 2 * WIDE, WIDE), bf16),
            pltpu.VMEM((max(levels, 1), tiles, 2 * WIDE, WIDE), bf16),
            pltpu.VMEM((max(levels, 1) * tiles, WIDE, WIDE), bf16),
            pltpu.VMEM((pieces, 2, HEAD_SIZE + TOTALS, WIDE), bf16),
            pltpu.VMEM((tiles, QUERY_HEADS, 8, WIDE), f32),
            pltpu.VMEM((tiles, QUERY_HEADS, HEAD_SIZE + TOTALS, WIDE), f32),
            pltpu.VMEM((rows, width), bf16),
            pltpu.SMEM(head_window_extent.shape, jnp.int32),
            pltpu.SMEM(block_mask.shape, jnp.int32),
            pltpu.SemaphoreType.DMA((9,)),
            pltpu.SemaphoreType.DMA((3,)),
            pltpu.SemaphoreType.DMA((4 + levels * tiles,)),
            pltpu.SemaphoreType.REGULAR((max(levels - 1, 1),)),
        ],
        compiler_params=pltpu.CompilerParams(
            collective_id=0, has_side_effects=True
        ),
    )(
        layer_queries, layer_keyvals, residual, head_window_extent, block_mask,
        first_out, second_query, second_keyval, second_out,
    )
    return pl.pallas_call(
        project,
        name="project",
        out_shape=jax.ShapeDtypeStruct((rows, width), bf16),
        in_specs=[held] * 3,
        out_specs=pl.BlockSpec(memory_space=pl.ANY),
        scratch_shapes=[
            pltpu.VMEM((rows, width), bf16),
            pltpu.SemaphoreType.DMA((max(1, width // (4 * WIDE)),)),
        ],
        compiler_params=pltpu.CompilerParams(vmem_limit_bytes=16 * 2**20),
    )(*(pltpu.with_memory_space_constraint(x, pltpu.VMEM) for x in (att, hidden, weights)))


def solution(mesh):
    placed = (
        P(("groups", "seq"), None),
        P(("groups", "seq"), None),
        P(("groups", "seq"), None),
        P(),
        P("seq", None),
        P(),
        P(),
        P(),
        P(),
    )
    return jax.shard_map(
        functools.partial(shards, mesh.shape["seq"]),
        mesh=mesh, in_specs=placed, out_specs=P(("groups", "seq"), None), check_vma=False,
    )
```

```python
import functools

import jax
import jax.numpy as jnp
from jax import lax
from jax.experimental import pallas as pl
from jax.experimental.pallas import tpu as pltpu
from jax.sharding import PartitionSpec as P

QUERY_HEADS = 8
HEAD_SIZE = 64
WIDE = 2 * HEAD_SIZE
MESH = pl.DeviceIdType.MESH
HIDE = -1e30
TOTALS = 16


def dot(a, b):
    return jnp.dot(a, b, preferred_element_type=jnp.float32)


def col_max(parts):
    top = jnp.max(parts[0], axis=0, keepdims=True)
    for part in parts[1:]:
        top = jnp.maximum(top, jnp.max(part, axis=0, keepdims=True))
    return top


def weight(scores, top):
    return jnp.exp((scores - top).astype(jnp.bfloat16))


def staggered(steps, scores, weigh, finish):
    ready, weighed = {}, {}
    count = len(steps)
    for at in range(count + 2):
        if at < count:
            ready[at] = scores(steps[at])
        if 0 <= at - 1 < count:
            weighed[at - 1] = weigh(steps[at - 1], ready.pop(at - 1))
        if 0 <= at - 2 < count:
            finish(steps[at - 2], *weighed.pop(at - 2))


def shared(acc):
    return acc[:HEAD_SIZE] * (1.0 / acc[HEAD_SIZE : HEAD_SIZE + 1])


def body(
    n, levels,
    q_hbm, kv_hbm, res_hbm, extent_hbm, mask_hbm, wo1_hbm, wq2_hbm, wkv2_hbm, wo2_hbm,
    att, hid, wo2,
    q, kv, res, wo1, wq2, wkv2, qx, halo, own2, came, kb, vt, tops, accs, norm,
    extent, mask, local_sem, send_sem, recv_sem, enter_sem,
):
    rows = q.shape[0]
    tiles = rows // WIDE
    pairs = q.shape[1] // WIDE
    group_heads = pairs
    heads = list(range(2 * pairs))
    bf16, f32 = jnp.bfloat16, jnp.float32
    scaled = bf16(HEAD_SIZE ** (-0.5))
    me = lax.axis_index("seq")
    loads = {
        name: pltpu.make_async_copy(src, dst, local_sem.at[i])
        for i, (name, src, dst) in enumerate(
            (
                ("kv", kv_hbm, kv),
                ("q", q_hbm, q),
                ("extent", extent_hbm, extent),
                ("mask", mask_hbm, mask),
                ("wo1", wo1_hbm, wo1),
                ("res", res_hbm, res),
                ("wkv2", wkv2_hbm, wkv2),
                ("wq2", wq2_hbm, wq2),
                ("wo2", wo2_hbm, wo2),
            )
        )
    }
    barrier = pltpu.get_barrier_semaphore()
    has_left, has_right = me > 0, me < n - 1

    def partner(level):
        bit = lax.rem(lax.div(me, 1 << level), 2)
        return me + (1 << level) * (1 - 2 * bit)

    def tell(sem, reach):
        @pl.when(me >= reach)
        def _():
            pl.semaphore_signal(sem, inc=1, device_id={"seq": me - reach}, device_id_type=MESH)

        @pl.when(me < n - reach)
        def _():
            pl.semaphore_signal(sem, inc=1, device_id={"seq": me + reach}, device_id_type=MESH)

    def told(sem, reach):
        pl.semaphore_wait(sem, (me >= reach).astype(jnp.int32) + (me < n - reach).astype(jnp.int32))

    tell(barrier, 1)
    for load in loads.values():
        load.start()

    def to_right(near):
        slot = 1 if near else 0
        return pltpu.make_async_remote_copy(
            kv_hbm.at[pl.ds(slot * WIDE, WIDE)], halo.at[slot], send_sem.at[0], recv_sem.at[slot],
            device_id={"seq": me + 1}, device_id_type=MESH,
        )

    def to_left(near):
        slot = 2 if near else 3
        return pltpu.make_async_remote_copy(
            kv_hbm.at[pl.ds((slot - 2) * WIDE, WIDE)], halo.at[slot], send_sem.at[1], recv_sem.at[slot],
            device_id={"seq": me - 1}, device_id_type=MESH,
        )

    told(barrier, 1)
    def send_halo(near):
        @pl.when(has_right)
        def _():
            to_right(near).start()

        @pl.when(has_left)
        def _():
            to_left(near).start()

    send_halo(True)

    stages = max(levels - 1, 0)

    def go_on(stage):
        if stage < stages:
            told(enter_sem.at[stage], 1 << stage)
            if stage + 1 < stages:
                tell(enter_sem.at[stage + 1], 1 << (stage + 1))

    if stages:
        tell(enter_sem.at[0], 1)

    for piece in range(vt.shape[0]):
        for group in range(2):
            vt[piece, group, HEAD_SIZE:] = jnp.ones((TOTALS, WIDE), bf16)

    @pl.when(jnp.logical_not(has_left))
    def _():
        halo[0:2] = jnp.zeros((2, *halo.shape[1:]), bf16)

    @pl.when(jnp.logical_not(has_right))
    def _():
        halo[2:4] = jnp.zeros((2, *halo.shape[1:]), bf16)

    def values_in(piece, turned):
        for group in range(2):
            vt[piece, group, :HEAD_SIZE] = turned[group * HEAD_SIZE : (group + 1) * HEAD_SIZE]

    def spread_queries(block):
        for pair in range(pairs):
            for t in range(tiles):
                turned = block[t * WIDE : (t + 1) * WIDE, pair * WIDE : (pair + 1) * WIDE].T
                for h in (2 * pair, 2 * pair + 1):
                    group = h // group_heads
                    start = group * HEAD_SIZE
                    qx[t, h, start : start + HEAD_SIZE] = turned[h % 2 * HEAD_SIZE : (h % 2 + 1) * HEAD_SIZE]

    for h in heads:
        start = (1 - h // group_heads) * HEAD_SIZE
        qx[:, h, start : start + HEAD_SIZE] = jnp.zeros((tiles, HEAD_SIZE, WIDE), bf16)

    def queries_of(h):
        return jnp.concatenate([qx[t, h] for t in range(tiles)], axis=1)

    loads["kv"].wait()
    for t in range(tiles):
        values_in(t, kv[t * WIDE : (t + 1) * WIDE, WIDE:].T)
    loads["q"].wait()
    loads["extent"].wait()
    loads["mask"].wait()
    spread_queries(q[...] * scaled)
    send_halo(False)

    def both(pieces, ref, group):
        return jnp.concatenate([ref[p, group] for p in pieces], axis=1)

    key = lax.broadcasted_iota(jnp.int32, (rows, rows), 0)
    query = lax.broadcasted_iota(jnp.int32, (rows, rows), 1)
    apart = jnp.abs(key - query)

    def own_scores(h):
        return (dot(kv[:, :WIDE], queries_of(h)),)

    def own_weigh(h, parts):
        scores = jnp.where(apart <= extent[h], parts[0], HIDE)
        top = col_max([scores])
        for t in range(tiles):
            tops[t, h] = jnp.broadcast_to(top[:, t * WIDE : (t + 1) * WIDE], tops.shape[2:])
        return (weight(scores, top),)

    def own_finish(h, shares):
        acc = dot(both(range(tiles), vt, h // group_heads), shares)
        for t in range(tiles):
            accs[t, h] = acc[:, t * WIDE : (t + 1) * WIDE]

    half = len(heads) // 2
    staggered(heads[:half], own_scores, own_weigh, own_finish)
    go_on(0)
    staggered(heads[half:], own_scores, own_weigh, own_finish)
    go_on(1)

    @pl.when(has_left)
    def _():
        to_right(True).wait_recv()

    @pl.when(has_right)
    def _():
        to_left(True).wait_recv()

    for piece in (1, 2):
        values_in(tiles + piece, halo[piece, :, WIDE:].T)

    parity = lax.rem(me, 2)
    order = (1 - parity, parity)
    far = 4 * n * rows
    left_off = jnp.where(has_left, 0, far)
    right_off = jnp.where(has_right, 0, far)
    delta = (
        lax.broadcasted_iota(jnp.int32, (WIDE, WIDE), 1)
        - lax.broadcasted_iota(jnp.int32, (WIDE, WIDE), 0)
    )
    single = max(levels - 2, 1)

    def landing(level, t):
        return 4 + level if level < single else 4 + single + (level - single) * tiles + t

    swaps = [
        [
            pltpu.make_async_remote_copy(
                own2.at[t], came.at[level, t],
                send_sem.at[2], recv_sem.at[landing(level, t)],
                device_id={"seq": partner(level)}, device_id_type=MESH,
            )
            for t in order
        ]
        for level in range(levels)
    ]
    halves = []

    def put(h, share, where_to):
        halves.append(share)
        if h % 2:
            pair = jnp.concatenate(halves, axis=0).astype(bf16)
            att[where_to, h // 2 * WIDE : (h // 2 + 1) * WIDE] = pair.T
            halves.clear()

    for name in ("wo1", "res", "wkv2"):
        loads[name].wait()
    for step, t in enumerate(order):
        here = pl.ds(pl.multiple_of(t * WIDE, WIDE), WIDE)
        at_left = t == 0

        @pl.when(jnp.logical_and(at_left, has_left))
        def _():
            to_right(False).wait_recv()

        @pl.when(jnp.logical_and(jnp.logical_not(at_left), has_right))
        def _():
            to_left(False).wait_recv()

        far_piece = 3 * t
        values_in(tiles + far_piece, halo[far_piece, :, WIDE:].T)
        sign = 1 - 2 * t
        off_mid = jnp.where(at_left, left_off, right_off)
        middle = delta * sign

        def twice(ref, h):
            return jnp.concatenate([ref[t, h], ref[t, h + 1]], axis=1)

        def side_scores(h):
            keys = jnp.concatenate([halo[t + i, :, :WIDE] for i in range(3)], axis=0)
            scores = dot(keys, twice(qx, h))
            return [scores[i * WIDE : (i + 1) * WIDE] for i in range(3)]

        def side_weigh(h, parts):
            kept = []
            for k in range(2):
                reach = extent[h + k]
                a, b, c = (part[:, k * WIDE : (k + 1) * WIDE] for part in parts)
                kept.append((
                    jnp.where(delta <= reach - rows - left_off, a, HIDE),
                    jnp.where(middle <= reach - WIDE - off_mid, b, HIDE),
                    jnp.where(delta >= rows + right_off - reach, c, HIDE),
                ))
            shares, fades = [], []
            for k in range(2):
                before = tops[t, h + k, 0:1]
                top = jnp.maximum(before, col_max(kept[k]))
                fades.append(jnp.exp(before - top))
                shares.append(jnp.concatenate([weight(x, top) for x in kept[k]], axis=0))
            return jnp.concatenate(fades, axis=1), jnp.concatenate(shares, axis=1)

        def side_finish(h, fade, shares):
            lhs = both([tiles + t + i for i in range(3)], vt, h // group_heads)
            acc = twice(accs, h) * fade + dot(lhs, shares)
            for k in range(2):
                put(h + k, shared(acc[:, k * WIDE : (k + 1) * WIDE]), here)

        staggered(heads[::2], side_scores, side_weigh, side_finish)

        hidden = (dot(att[here], wo1[...]) + res[here].astype(f32)).astype(bf16)
        hid[here] = hidden
        values = hidden.astype(f32)
        scale = lax.rsqrt(jnp.mean(values * values, axis=-1, keepdims=True) + 1e-05)
        normed = (values * scale).astype(bf16)
        norm[here] = normed
        keyvals = dot(normed, wkv2[...]).astype(bf16)
        own2[t, :WIDE] = keyvals[:, :WIDE]
        own2[t, WIDE:] = keyvals[:, WIDE:].T
        if step == 0:
            for stage in range(2, stages):
                go_on(stage)
        for swap in reversed(swaps):
            swap[step].start()

    loads["wq2"].wait()
    spread_queries(dot(norm[...], wq2[...]).astype(bf16) * scaled)

    first = [(0, t) for t in range(tiles)]
    chunks = [first]
    if levels > 0:
        chunks = [first + [(1, t) for t in range(tiles)]]
    a, b = order
    later = [(level + 1, t) for level in range(1, levels - 2) for t in order]
    if levels > 2:
        later.append((levels - 1, a))
    chunks += [later[i : i + 3] for i in range(0, len(later), 3)]
    if levels > 2:
        chunks += [[(levels, a), (levels - 1, b)], [(levels, b)]]
    elif levels == 2:
        chunks += [[(levels, a)], [(levels, b)]]
    last = len(chunks) - 1
    landed = set()

    for number, chunk in enumerate(chunks):
        for slot, t in chunk:
            if slot == 0:
                values_in(t, own2[t, WIDE:])
                continue
            level = slot - 1
            if level >= single or level not in landed:
                here = came.at[level] if level < single else came.at[level, t]
                pltpu.make_async_remote_copy(
                    here, here, send_sem.at[2], recv_sem.at[landing(level, t)],
                    device_id={"seq": partner(level)}, device_id_type=MESH,
                ).wait_recv()
                landed.add(level)
            seen = mask[0, level] == 1
            piece = slot * tiles + t
            kb[level * tiles + t] = jnp.where(seen, came[level, t, :WIDE], own2[t, :WIDE])
            turned = came[level, t, WIDE:]
            values_in(piece, jnp.where(seen, turned, jnp.zeros_like(turned)))
            for group in range(2):
                vt[piece, group, HEAD_SIZE:] = jnp.where(
                    seen, jnp.ones((TOTALS, WIDE), bf16), jnp.zeros((TOTALS, WIDE), bf16)
                )

        def keys_of(slot, t):
            return own2[t, :WIDE] if slot == 0 else kb[(slot - 1) * tiles + t]

        def far_scores(h):
            keys = jnp.concatenate([keys_of(slot, t) for slot, t in chunk], axis=0)
            scores = dot(keys, queries_of(h))
            return [scores[i * WIDE : (i + 1) * WIDE] for i in range(len(chunk))]

        def far_weigh(h, parts):
            top = col_max(parts)
            fade = None
            if number > 0:
                before = jnp.concatenate([tops[t, h, 0:1] for t in range(tiles)], axis=1)
                top = jnp.maximum(before, top)
                fade = jnp.exp(before - top)
            if number < last:
                for t in range(tiles):
                    tops[t, h] = jnp.broadcast_to(top[:, t * WIDE : (t + 1) * WIDE], tops.shape[2:])
            return fade, [weight(part, top) for part in parts]

        def far_finish(h, fade, parts):
            acc = None
            if fade is not None:
                acc = jnp.concatenate([accs[t, h] for t in range(tiles)], axis=1) * fade
            for i in range(0, len(chunk), 2):
                lhs = both([slot * tiles + t for slot, t in chunk[i : i + 2]], vt, h // group_heads)
                term = dot(lhs, jnp.concatenate(parts[i : i + 2], axis=0))
                acc = term if acc is None else acc + term
            if number < last:
                for t in range(tiles):
                    accs[t, h] = acc[:, t * WIDE : (t + 1) * WIDE]
            else:
                put(h, shared(acc), slice(0, rows))

        staggered(heads, far_scores, far_weigh, far_finish)

    loads["wo2"].wait()
    def sent(sem, whole):
        pltpu.make_async_remote_copy(
            whole, whole, send_sem.at[sem], recv_sem.at[0],
            device_id={"seq": partner(0)}, device_id_type=MESH,
        ).wait_send()

    if levels:
        sent(2, came)

    @pl.when(has_right)
    def _():
        sent(0, halo.at[pl.ds(0, 2)])

    @pl.when(has_left)
    def _():
        sent(1, halo.at[pl.ds(0, 2)])


def project(att, hid, weight_ref, out_hbm, out, sem):
    width = out.shape[1]
    step = min(width, 4 * WIDE)
    copies = []
    for start in range(0, width, step):
        here = pl.ds(start, step)
        total = dot(att[...], weight_ref[:, here]) + hid[:, here].astype(jnp.float32)
        out[:, here] = total.astype(out.dtype)
        copies.append(pltpu.make_async_copy(out.at[:, here], out_hbm.at[:, here], sem.at[len(copies)]))
        copies[-1].start()
    for copy in copies:
        copy.wait()


def shards(
    n, residual, layer_queries, layer_keyvals, head_window_extent, block_mask,
    first_out, second_query, second_keyval, second_out,
):
    levels = n.bit_length() - 1
    rows, width = residual.shape
    query_width = layer_queries.shape[1]
    kv_width = layer_keyvals.shape[1]
    tiles = rows // WIDE
    pieces = max(tiles + 4, (levels + 1) * tiles)
    bf16, f32 = jnp.bfloat16, jnp.float32
    stays = pl.BlockSpec(memory_space=pltpu.HBM)
    held = pl.BlockSpec(memory_space=pltpu.VMEM)
    att, hidden, weights = pl.pallas_call(
        functools.partial(body, n, levels),
        name="two_layers",
        out_shape=(
            pltpu.VMEM((rows, query_width), bf16),
            pltpu.VMEM((rows, width), bf16),
            pltpu.VMEM(second_out.shape, bf16),
        ),
        in_specs=[stays] * 9,
        out_specs=(held, held, held),
        scratch_shapes=[
            pltpu.VMEM((rows, query_width), bf16),
            pltpu.VMEM((rows, kv_width), bf16),
            pltpu.VMEM((rows, width), bf16),
            pltpu.VMEM(first_out.shape, bf16),
            pltpu.VMEM(second_query.shape, bf16),
            pltpu.VMEM(second_keyval.shape, bf16),
            pltpu.VMEM((tiles, QUERY_HEADS, WIDE, WIDE), bf16),
            pltpu.VMEM((4, WIDE, kv_width), bf16),
            pltpu.VMEM((tiles, 2 * WIDE, WIDE), bf16),
            pltpu.VMEM((max(levels, 1), tiles, 2 * WIDE, WIDE), bf16),
            pltpu.VMEM((max(levels, 1) * tiles, WIDE, WIDE), bf16),
            pltpu.VMEM((pieces, 2, HEAD_SIZE + TOTALS, WIDE), bf16),
            pltpu.VMEM((tiles, QUERY_HEADS, 8, WIDE), f32),
            pltpu.VMEM((tiles, QUERY_HEADS, HEAD_SIZE + TOTALS, WIDE), f32),
            pltpu.VMEM((rows, width), bf16),
            pltpu.SMEM(head_window_extent.shape, jnp.int32),
            pltpu.SMEM(block_mask.shape, jnp.int32),
            pltpu.SemaphoreType.DMA((9,)),
            pltpu.SemaphoreType.DMA((3,)),
            pltpu.SemaphoreType.DMA((4 + levels * tiles,)),
            pltpu.SemaphoreType.REGULAR((max(levels - 1, 1),)),
        ],
        compiler_params=pltpu.CompilerParams(
            collective_id=0, has_side_effects=True
        ),
    )(
        layer_queries, layer_keyvals, residual, head_window_extent, block_mask,
        first_out, second_query, second_keyval, second_out,
    )
    return pl.pallas_call(
        project,
        name="project",
        out_shape=jax.ShapeDtypeStruct((rows, width), bf16),
        in_specs=[held] * 3,
        out_specs=pl.BlockSpec(memory_space=pl.ANY),
        scratch_shapes=[
            pltpu.VMEM((rows, width), bf16),
            pltpu.SemaphoreType.DMA((max(1, width // (4 * WIDE)),)),
        ],
        compiler_params=pltpu.CompilerParams(vmem_limit_bytes=16 * 2**20),
    )(*(pltpu.with_memory_space_constraint(x, pltpu.VMEM) for x in (att, hidden, weights)))


def solution(mesh):
    placed = (
        P(("groups", "seq"), None),
        P(("groups", "seq"), None),
        P(("groups", "seq"), None),
        P(),
        P("seq", None),
        P(),
        P(),
        P(),
        P(),
    )
    return jax.shard_map(
        functools.partial(shards, mesh.shape["seq"]),
        mesh=mesh, in_specs=placed, out_specs=P(("groups", "seq"), None), check_vma=False,
    )
```

```python
import functools

import jax
import jax.numpy as jnp
from jax import lax
from jax.experimental import pallas as pl
from jax.experimental.pallas import tpu as pltpu
from jax.sharding import PartitionSpec as P

QUERY_HEADS = 8
HEAD_SIZE = 64
WIDE = 2 * HEAD_SIZE
MESH = pl.DeviceIdType.MESH
HIDE = -1e30
TOTALS = 16


def dot(a, b):
    return jnp.dot(a, b, preferred_element_type=jnp.float32)


def col_max(parts):
    top = jnp.max(parts[0], axis=0, keepdims=True)
    for part in parts[1:]:
        top = jnp.maximum(top, jnp.max(part, axis=0, keepdims=True))
    return top


def weight(scores, top):
    return jnp.exp((scores - top).astype(jnp.bfloat16))


def staggered(steps, scores, weigh, finish):
    ready, weighed = {}, {}
    count = len(steps)
    for at in range(count + 2):
        if at < count:
            ready[at] = scores(steps[at])
        if 0 <= at - 1 < count:
            weighed[at - 1] = weigh(steps[at - 1], ready.pop(at - 1))
        if 0 <= at - 2 < count:
            finish(steps[at - 2], *weighed.pop(at - 2))


def shared(acc):
    return acc[:HEAD_SIZE] * (1.0 / acc[HEAD_SIZE : HEAD_SIZE + 1])


def body(
    n, levels,
    q_hbm, kv_hbm, res_hbm, extent_hbm, mask_hbm, wo1_hbm, wq2_hbm, wkv2_hbm, wo2_hbm,
    att, hid, wo2,
    q, kv, res, wo1, wq2, wkv2, qx, halo, own2, came, kb, vt, tops, accs, norm,
    extent, mask, local_sem, send_sem, recv_sem, enter_sem,
):
    rows = q.shape[0]
    tiles = rows // WIDE
    pairs = q.shape[1] // WIDE
    group_heads = pairs
    heads = list(range(2 * pairs))
    bf16, f32 = jnp.bfloat16, jnp.float32
    scaled = bf16(HEAD_SIZE ** (-0.5))
    me = lax.axis_index("seq")
    loads = {
        name: pltpu.make_async_copy(src, dst, local_sem.at[i])
        for i, (name, src, dst) in enumerate(
            (
                ("kv", kv_hbm, kv),
                ("q", q_hbm, q),
                ("extent", extent_hbm, extent),
                ("mask", mask_hbm, mask),
                ("wo1", wo1_hbm, wo1),
                ("res", res_hbm, res),
                ("wkv2", wkv2_hbm, wkv2),
                ("wq2", wq2_hbm, wq2),
                ("wo2", wo2_hbm, wo2),
            )
        )
    }
    barrier = pltpu.get_barrier_semaphore()
    has_left, has_right = me > 0, me < n - 1

    def partner(level):
        bit = lax.rem(lax.div(me, 1 << level), 2)
        return me + (1 << level) * (1 - 2 * bit)

    def tell(sem, reach):
        @pl.when(me >= reach)
        def _():
            pl.semaphore_signal(sem, inc=1, device_id={"seq": me - reach}, device_id_type=MESH)

        @pl.when(me < n - reach)
        def _():
            pl.semaphore_signal(sem, inc=1, device_id={"seq": me + reach}, device_id_type=MESH)

    def told(sem, reach):
        pl.semaphore_wait(sem, (me >= reach).astype(jnp.int32) + (me < n - reach).astype(jnp.int32))

    tell(barrier, 1)
    for load in loads.values():
        load.start()

    def to_right(near):
        slot = 1 if near else 0
        return pltpu.make_async_remote_copy(
            kv_hbm.at[pl.ds(slot * WIDE, WIDE)], halo.at[slot], send_sem.at[0], recv_sem.at[slot],
            device_id={"seq": me + 1}, device_id_type=MESH,
        )

    def to_left(near):
        slot = 2 if near else 3
        return pltpu.make_async_remote_copy(
            kv_hbm.at[pl.ds((slot - 2) * WIDE, WIDE)], halo.at[slot], send_sem.at[1], recv_sem.at[slot],
            device_id={"seq": me - 1}, device_id_type=MESH,
        )

    told(barrier, 1)
    def send_halo(near):
        @pl.when(has_right)
        def _():
            to_right(near).start()

        @pl.when(has_left)
        def _():
            to_left(near).start()

    send_halo(True)

    stages = max(levels - 1, 0)

    def go_on(stage):
        if stage < stages:
            told(enter_sem.at[stage], 1 << stage)
            if stage + 1 < stages:
                tell(enter_sem.at[stage + 1], 1 << (stage + 1))

    if stages:
        tell(enter_sem.at[0], 1)

    for piece in range(vt.shape[0]):
        for group in range(2):
            vt[piece, group, HEAD_SIZE:] = jnp.ones((TOTALS, WIDE), bf16)

    @pl.when(jnp.logical_not(has_left))
    def _():
        halo[0:2] = jnp.zeros((2, *halo.shape[1:]), bf16)

    @pl.when(jnp.logical_not(has_right))
    def _():
        halo[2:4] = jnp.zeros((2, *halo.shape[1:]), bf16)

    def values_in(piece, turned):
        for group in range(2):
            vt[piece, group, :HEAD_SIZE] = turned[group * HEAD_SIZE : (group + 1) * HEAD_SIZE]

    def spread_queries(block):
        for pair in range(pairs):
            for t in range(tiles):
                turned = block[t * WIDE : (t + 1) * WIDE, pair * WIDE : (pair + 1) * WIDE].T
                for h in (2 * pair, 2 * pair + 1):
                    group = h // group_heads
                    start = group * HEAD_SIZE
                    qx[t, h, start : start + HEAD_SIZE] = turned[h % 2 * HEAD_SIZE : (h % 2 + 1) * HEAD_SIZE]

    for h in heads:
        start = (1 - h // group_heads) * HEAD_SIZE
        qx[:, h, start : start + HEAD_SIZE] = jnp.zeros((tiles, HEAD_SIZE, WIDE), bf16)

    def queries_of(h):
        return jnp.concatenate([qx[t, h] for t in range(tiles)], axis=1)

    loads["kv"].wait()
    for t in range(tiles):
        values_in(t, kv[t * WIDE : (t + 1) * WIDE, WIDE:].T)
    loads["q"].wait()
    loads["extent"].wait()
    loads["mask"].wait()
    spread_queries(q[...] * scaled)
    send_halo(False)

    def both(pieces, ref, group):
        return jnp.concatenate([ref[p, group] for p in pieces], axis=1)

    key = lax.broadcasted_iota(jnp.int32, (rows, rows), 0)
    query = lax.broadcasted_iota(jnp.int32, (rows, rows), 1)
    apart = jnp.abs(key - query)

    def own_scores(h):
        return (dot(kv[:, :WIDE], queries_of(h)),)

    def own_weigh(h, parts):
        scores = jnp.where(apart <= extent[h], parts[0], HIDE)
        top = col_max([scores])
        for t in range(tiles):
            tops[t, h] = jnp.broadcast_to(top[:, t * WIDE : (t + 1) * WIDE], tops.shape[2:])
        return (weight(scores, top),)

    def own_finish(h, shares):
        acc = dot(both(range(tiles), vt, h // group_heads), shares)
        for t in range(tiles):
            accs[t, h] = acc[:, t * WIDE : (t + 1) * WIDE]

    half = len(heads) // 2
    staggered(heads[:half], own_scores, own_weigh, own_finish)
    go_on(0)
    staggered(heads[half:], own_scores, own_weigh, own_finish)
    go_on(1)

    @pl.when(has_left)
    def _():
        to_right(True).wait_recv()

    @pl.when(has_right)
    def _():
        to_left(True).wait_recv()

    for piece in (1, 2):
        values_in(tiles + piece, halo[piece, :, WIDE:].T)

    parity = lax.rem(me, 2)
    order = (1 - parity, parity)
    far = 4 * n * rows
    left_off = jnp.where(has_left, 0, far)
    right_off = jnp.where(has_right, 0, far)
    delta = (
        lax.broadcasted_iota(jnp.int32, (WIDE, WIDE), 1)
        - lax.broadcasted_iota(jnp.int32, (WIDE, WIDE), 0)
    )
    swaps = [
        [
            pltpu.make_async_remote_copy(
                own2.at[t], came.at[level, t],
                send_sem.at[2], recv_sem.at[4 + level * tiles + t],
                device_id={"seq": partner(level)}, device_id_type=MESH,
            )
            for t in order
        ]
        for level in range(levels)
    ]
    halves = []

    def put(h, share, where_to):
        halves.append(share)
        if h % 2:
            pair = jnp.concatenate(halves, axis=0).astype(bf16)
            att[where_to, h // 2 * WIDE : (h // 2 + 1) * WIDE] = pair.T
            halves.clear()

    for name in ("wo1", "res", "wkv2"):
        loads[name].wait()
    for step, t in enumerate(order):
        here = pl.ds(pl.multiple_of(t * WIDE, WIDE), WIDE)
        at_left = t == 0

        @pl.when(jnp.logical_and(at_left, has_left))
        def _():
            to_right(False).wait_recv()

        @pl.when(jnp.logical_and(jnp.logical_not(at_left), has_right))
        def _():
            to_left(False).wait_recv()

        far_piece = 3 * t
        values_in(tiles + far_piece, halo[far_piece, :, WIDE:].T)
        sign = 1 - 2 * t
        off_mid = jnp.where(at_left, left_off, right_off)
        middle = delta * sign

        def twice(ref, h):
            return jnp.concatenate([ref[t, h], ref[t, h + 1]], axis=1)

        def side_scores(h):
            keys = jnp.concatenate([halo[t + i, :, :WIDE] for i in range(3)], axis=0)
            scores = dot(keys, twice(qx, h))
            return [scores[i * WIDE : (i + 1) * WIDE] for i in range(3)]

        def side_weigh(h, parts):
            kept = []
            for k in range(2):
                reach = extent[h + k]
                a, b, c = (part[:, k * WIDE : (k + 1) * WIDE] for part in parts)
                kept.append((
                    jnp.where(delta <= reach - rows - left_off, a, HIDE),
                    jnp.where(middle <= reach - WIDE - off_mid, b, HIDE),
                    jnp.where(delta >= rows + right_off - reach, c, HIDE),
                ))
            shares, fades = [], []
            for k in range(2):
                before = tops[t, h + k, 0:1]
                top = jnp.maximum(before, col_max(kept[k]))
                fades.append(jnp.exp(before - top))
                shares.append(jnp.concatenate([weight(x, top) for x in kept[k]], axis=0))
            return jnp.concatenate(fades, axis=1), jnp.concatenate(shares, axis=1)

        def side_finish(h, fade, shares):
            lhs = both([tiles + t + i for i in range(3)], vt, h // group_heads)
            acc = twice(accs, h) * fade + dot(lhs, shares)
            for k in range(2):
                put(h + k, shared(acc[:, k * WIDE : (k + 1) * WIDE]), here)

        staggered(heads[::2], side_scores, side_weigh, side_finish)

        hidden = (dot(att[here], wo1[...]) + res[here].astype(f32)).astype(bf16)
        hid[here] = hidden
        values = hidden.astype(f32)
        scale = lax.rsqrt(jnp.mean(values * values, axis=-1, keepdims=True) + 1e-05)
        normed = (values * scale).astype(bf16)
        norm[here] = normed
        keyvals = dot(normed, wkv2[...]).astype(bf16)
        own2[t, :WIDE] = keyvals[:, :WIDE]
        own2[t, WIDE:] = keyvals[:, WIDE:].T
        if step == 0:
            for stage in range(2, stages):
                go_on(stage)
        for swap in reversed(swaps):
            swap[step].start()

    loads["wq2"].wait()
    spread_queries(dot(norm[...], wq2[...]).astype(bf16) * scaled)

    first = [(0, t) for t in range(tiles)]
    chunks = [first]
    if levels > 0:
        chunks = [first + [(1, t) for t in range(tiles)]]
    a, b = order
    later = [(level + 1, t) for level in range(1, levels - 2) for t in order]
    if levels > 2:
        later.append((levels - 1, a))
    chunks += [later[i : i + 3] for i in range(0, len(later), 3)]
    if levels > 2:
        chunks += [[(levels, a), (levels - 1, b)], [(levels, b)]]
    elif levels == 2:
        chunks += [[(levels, a)], [(levels, b)]]
    last = len(chunks) - 1

    for number, chunk in enumerate(chunks):
        for slot, t in chunk:
            if slot == 0:
                values_in(t, own2[t, WIDE:])
                continue
            level = slot - 1
            pltpu.make_async_remote_copy(
                own2.at[t], came.at[level, t],
                send_sem.at[2], recv_sem.at[4 + level * tiles + t],
                device_id={"seq": partner(level)}, device_id_type=MESH,
            ).wait_recv()
            seen = mask[0, level] == 1
            piece = slot * tiles + t
            kb[level * tiles + t] = jnp.where(seen, came[level, t, :WIDE], own2[t, :WIDE])
            turned = came[level, t, WIDE:]
            values_in(piece, jnp.where(seen, turned, jnp.zeros_like(turned)))
            for group in range(2):
                vt[piece, group, HEAD_SIZE:] = jnp.where(
                    seen, jnp.ones((TOTALS, WIDE), bf16), jnp.zeros((TOTALS, WIDE), bf16)
                )

        def keys_of(slot, t):
            return own2[t, :WIDE] if slot == 0 else kb[(slot - 1) * tiles + t]

        def far_scores(h):
            keys = jnp.concatenate([keys_of(slot, t) for slot, t in chunk], axis=0)
            scores = dot(keys, queries_of(h))
            return [scores[i * WIDE : (i + 1) * WIDE] for i in range(len(chunk))]

        def far_weigh(h, parts):
            top = col_max(parts)
            fade = None
            if number > 0:
                before = jnp.concatenate([tops[t, h, 0:1] for t in range(tiles)], axis=1)
                top = jnp.maximum(before, top)
                fade = jnp.exp(before - top)
            if number < last:
                for t in range(tiles):
                    tops[t, h] = jnp.broadcast_to(top[:, t * WIDE : (t + 1) * WIDE], tops.shape[2:])
            return fade, [weight(part, top) for part in parts]

        def far_finish(h, fade, parts):
            acc = None
            if fade is not None:
                acc = jnp.concatenate([accs[t, h] for t in range(tiles)], axis=1) * fade
            for i in range(0, len(chunk), 2):
                lhs = both([slot * tiles + t for slot, t in chunk[i : i + 2]], vt, h // group_heads)
                term = dot(lhs, jnp.concatenate(parts[i : i + 2], axis=0))
                acc = term if acc is None else acc + term
            if number < last:
                for t in range(tiles):
                    accs[t, h] = acc[:, t * WIDE : (t + 1) * WIDE]
            else:
                put(h, shared(acc), slice(0, rows))

        staggered(heads, far_scores, far_weigh, far_finish)

    loads["wo2"].wait()
    def sent(sem, whole):
        pltpu.make_async_remote_copy(
            whole, whole, send_sem.at[sem], recv_sem.at[0],
            device_id={"seq": partner(0)}, device_id_type=MESH,
        ).wait_send()

    if levels:
        sent(2, came)

    @pl.when(has_right)
    def _():
        sent(0, halo.at[pl.ds(0, 2)])

    @pl.when(has_left)
    def _():
        sent(1, halo.at[pl.ds(0, 2)])


def project(att, hid, weight_ref, out_hbm, out, sem):
    width = out.shape[1]
    last = min(width, 2 * WIDE)
    copies = []
    for start, size in ((0, width - last), (width - last, last)):
        if size == 0:
            continue
        here = pl.ds(start, size)
        total = dot(att[...], weight_ref[:, here]) + hid[:, here].astype(jnp.float32)
        out[:, here] = total.astype(out.dtype)
        copies.append(pltpu.make_async_copy(out.at[:, here], out_hbm.at[:, here], sem.at[len(copies)]))
        copies[-1].start()
    for copy in copies:
        copy.wait()


def shards(
    n, residual, layer_queries, layer_keyvals, head_window_extent, block_mask,
    first_out, second_query, second_keyval, second_out,
):
    levels = n.bit_length() - 1
    rows, width = residual.shape
    query_width = layer_queries.shape[1]
    kv_width = layer_keyvals.shape[1]
    tiles = rows // WIDE
    pieces = max(tiles + 4, (levels + 1) * tiles)
    bf16, f32 = jnp.bfloat16, jnp.float32
    stays = pl.BlockSpec(memory_space=pltpu.HBM)
    held = pl.BlockSpec(memory_space=pltpu.VMEM)
    att, hidden, weights = pl.pallas_call(
        functools.partial(body, n, levels),
        name="two_layers",
        out_shape=(
            pltpu.VMEM((rows, query_width), bf16),
            pltpu.VMEM((rows, width), bf16),
            pltpu.VMEM(second_out.shape, bf16),
        ),
        in_specs=[stays] * 9,
        out_specs=(held, held, held),
        scratch_shapes=[
            pltpu.VMEM((rows, query_width), bf16),
            pltpu.VMEM((rows, kv_width), bf16),
            pltpu.VMEM((rows, width), bf16),
            pltpu.VMEM(first_out.shape, bf16),
            pltpu.VMEM(second_query.shape, bf16),
            pltpu.VMEM(second_keyval.shape, bf16),
            pltpu.VMEM((tiles, QUERY_HEADS, WIDE, WIDE), bf16),
            pltpu.VMEM((4, WIDE, kv_width), bf16),
            pltpu.VMEM((tiles, 2 * WIDE, WIDE), bf16),
            pltpu.VMEM((max(levels, 1), tiles, 2 * WIDE, WIDE), bf16),
            pltpu.VMEM((max(levels, 1) * tiles, WIDE, WIDE), bf16),
            pltpu.VMEM((pieces, 2, HEAD_SIZE + TOTALS, WIDE), bf16),
            pltpu.VMEM((tiles, QUERY_HEADS, 8, WIDE), f32),
            pltpu.VMEM((tiles, QUERY_HEADS, HEAD_SIZE + TOTALS, WIDE), f32),
            pltpu.VMEM((rows, width), bf16),
            pltpu.SMEM(head_window_extent.shape, jnp.int32),
            pltpu.SMEM(block_mask.shape, jnp.int32),
            pltpu.SemaphoreType.DMA((9,)),
            pltpu.SemaphoreType.DMA((3,)),
            pltpu.SemaphoreType.DMA((4 + levels * tiles,)),
            pltpu.SemaphoreType.REGULAR((max(levels - 1, 1),)),
        ],
        compiler_params=pltpu.CompilerParams(
            collective_id=0, has_side_effects=True
        ),
    )(
        layer_queries, layer_keyvals, residual, head_window_extent, block_mask,
        first_out, second_query, second_keyval, second_out,
    )
    return pl.pallas_call(
        project,
        name="project",
        out_shape=jax.ShapeDtypeStruct((rows, width), bf16),
        in_specs=[held] * 3,
        out_specs=pl.BlockSpec(memory_space=pl.ANY),
        scratch_shapes=[
            pltpu.VMEM((rows, width), bf16),
            pltpu.SemaphoreType.DMA((2,)),
        ],
        compiler_params=pltpu.CompilerParams(vmem_limit_bytes=16 * 2**20),
    )(*(pltpu.with_memory_space_constraint(x, pltpu.VMEM) for x in (att, hidden, weights)))


def solution(mesh):
    placed = (
        P(("groups", "seq"), None),
        P(("groups", "seq"), None),
        P(("groups", "seq"), None),
        P(),
        P("seq", None),
        P(),
        P(),
        P(),
        P(),
    )
    return jax.shard_map(
        functools.partial(shards, mesh.shape["seq"]),
        mesh=mesh, in_specs=placed, out_specs=P(("groups", "seq"), None), check_vma=False,
    )
```
